32 devices in a mesh: parts: 2 (over x), blk: 16 (over z, y, core).
Axes of the slice: x: 2, y: 2, z: 4, core: 2. Of those that a mesh axis runs over, the one named last changes fastest.
Arguments:
- observed: bfloat16 [24576, 1024], P(('parts', 'blk')), parts along dimension 0, may hold values from -6 to 6
- sharpness: float32 [24576], P(('parts', 'blk')), parts along dimension 0, may hold values from 0.03 to 0.15
- obs_class: int32 [24576], P(('parts', 'blk')), parts along dimension 0, may hold values from 0 to 7
- pattern: int32 [192, 16], P(('parts', 'blk')), parts along dimension 0, may hold values from 0 to 1, as said below
- evolved: bfloat16 [4096, 1024], P(('parts', 'blk')), parts along dimension 0, may hold values from -6 to 6
- sim_params: bfloat16 [4, 4096], P(None, ('parts', 'blk')), parts along dimension 1, may hold values from -6 to 6
- sim_class: int32 [4096], P(('parts', 'blk')), parts along dimension 0, may hold values from 0 to 7, as said below
Outputs:
- posterior_mean: float32 [4, 24576], P(None, ('parts', 'blk')), parts along dimension 1
- log_evidence: float32 [24576], P(('parts', 'blk')), parts along dimension 0
The draws below stay inside these ranges and needn't reach their ends.
There are 2 independent parts, one for each index of `parts`. The reference program is written for one: setup_inputs(seed, part) draws one part's arguments, and reference() takes and returns one part's arrays. A program takes and returns all parts, laid end to end along the dimension named above; each array names one. Nothing has to cross between parts.
Inputs may be any that keep to these rules, and one draw needn't show every extreme that they name: `sim_class`: every block of 128 evolved profiles holds every class, at its first 8 positions. `pattern`: every block of observed profiles is compared with at least one block of evolved profiles; the share of compared blocks differs from one observed block to another.
All inputs are finite; a program needn't handle non-finite values.
Results may differ from the reference program's by a relative error of at most 0.0045.
Values may be sent and summed in bfloat16 or wider, within the bound.
A program may use at most 64 MiB of HBM per device.

```python
import math
import jax
import jax.numpy as jnp
from jax import lax

P_SIZE = 1024
NPARAM = 4
NCLASS = 8
BLOCK = 128
NOBS = 12288
NSIM = 2048
OBS_BLOCKS = 96
SIM_BLOCKS = 16


def class_tables(key):
    key_sim = jax.random.fold_in(key, 101)
    key_obs = jax.random.fold_in(key, 102)
    key_level = jax.random.fold_in(key, 103)
    key_mask = jax.random.fold_in(key, 104)
    key_force = jax.random.fold_in(key, 105)
    sim_class = jax.random.randint(key_sim, (NSIM,), 0, NCLASS)
    within = jnp.arange(NSIM) % BLOCK
    sim_class = jnp.where(within < NCLASS, within, sim_class).astype(jnp.int32)
    obs_class = jax.random.randint(key_obs, (NOBS,), 0, NCLASS).astype(jnp.int32)
    levels = jax.random.randint(key_level, (OBS_BLOCKS, 1), 1, 9)
    rolls = jax.random.randint(key_mask, (OBS_BLOCKS, SIM_BLOCKS), 0, 16)
    forced = jax.random.randint(key_force, (OBS_BLOCKS, 1), 0, SIM_BLOCKS)
    opened = (rolls < levels) | (jnp.arange(SIM_BLOCKS)[None, :] == forced)
    return (obs_class, sim_class, opened.astype(jnp.int32))


def sim_values(key):
    key_base = jax.random.fold_in(key, 201)
    base = jax.random.normal(key_base, (NSIM, P_SIZE), jnp.float32)
    return jnp.clip(base, -6.0, 6.0)


def draw_obs_class(key, part):
    return class_tables(key)[0]


def draw_sim_class(key, part):
    return class_tables(key)[1]


def draw_pattern(key, part):
    return class_tables(key)[2]


def draw_evolved(key, part):
    return sim_values(key).astype(jnp.bfloat16)


def draw_observed(key, part):
    key_own = jax.random.fold_in(key, 301)
    base = jax.random.normal(key_own, (NOBS, P_SIZE), jnp.float32)
    return jnp.clip(base, -6.0, 6.0).astype(jnp.bfloat16)


def block_levels(rng, shape, shards, least, largest):
    factor_of = 1.0
    for dim, blocks in shards:
        draws = jax.random.uniform(jax.random.fold_in(jax.random.fold_in(rng, 6), dim), (blocks,), jnp.float32, least / len(shards), largest / len(shards))
        factor_of = factor_of * jnp.repeat(jnp.exp(draws), shape[dim] // blocks).reshape((-1,) + (1,) * (len(shape) - 1 - dim))
    return factor_of


def gaussian(key, dims, spread, limit, shards=(), held_as=jnp.bfloat16):
    gain = block_levels(key, dims, shards, -0.22, 0.18) if shards else 1.0
    array = jax.random.normal(key, dims, jnp.float32) * spread * gain
    return jnp.minimum(jnp.maximum(array, -limit), limit).astype(held_as)


def setup_inputs(seed: int = 0, part: int = 0) -> dict:
    splits = jax.random.split(jax.random.key(seed), 8)
    part_keys = jax.random.split(jax.random.fold_in(splits[7], part), 8)
    observed = draw_observed(jax.random.fold_in(jax.random.fold_in(splits[7], part), 71), part)
    sharpness = jnp.clip(jnp.exp(math.log(0.15) - 1.609438 * jax.random.uniform(part_keys[1], (NOBS,), jnp.float32) ** block_levels(part_keys[1], (NOBS,), ((0, 16),), -0.2, 0.2)), 0.03, 0.15)
    obs_class = draw_obs_class(jax.random.fold_in(jax.random.fold_in(splits[7], part), 71), part)
    pattern = draw_pattern(jax.random.fold_in(jax.random.fold_in(splits[7], part), 71), part)
    evolved = draw_evolved(jax.random.fold_in(jax.random.fold_in(splits[7], part), 71), part)
    sim_params = gaussian(part_keys[5], (NPARAM, NSIM), 1.0, 6.0, ((1, 16),))
    sim_class = draw_sim_class(jax.random.fold_in(jax.random.fold_in(splits[7], part), 71), part)
    return dict(observed=observed, sharpness=sharpness, obs_class=obs_class, pattern=pattern, evolved=evolved, sim_params=sim_params, sim_class=sim_class)


NEG_START = -1.0e30


def visit_block(observed, obs_sq, sharpness, obs_class, rows_open, sims, params, sims_class, running_max, weight_total, param_sums):
    sims_sq = jnp.sum(jnp.square(sims.astype(jnp.float32)), axis=1)
    inner = lax.dot_general(observed, sims, (((1,), (1,)), ((), ())), preferred_element_type=jnp.float32)
    distance = obs_sq[:, None] + sims_sq[None, :] - 2.0 * inner
    score = sharpness[:, None] * (2.0 * P_SIZE - distance)
    active = rows_open[:, None] & (obs_class[:, None] == sims_class[None, :])
    new_max = jnp.maximum(running_max, jnp.max(jnp.where(active, score, NEG_START), axis=1))
    factor = jnp.exp(running_max - new_max)
    weights = jnp.where(active, jnp.exp(score - new_max[:, None]), 0.0)
    weight_total = weight_total * factor + jnp.sum(weights, axis=1)
    weight_low = weights.astype(jnp.bfloat16)
    added = lax.dot_general(params, weight_low, (((1,), (1,)), ((), ())), preferred_element_type=jnp.float32)
    param_sums = param_sums * factor[None, :] + added
    return new_max, weight_total, param_sums


def reference(observed, sharpness, obs_class, pattern, evolved, sim_params, sim_class):
    obs_sq = jnp.sum(jnp.square(observed.astype(jnp.float32)), axis=1)
    row_block = (jnp.arange(NOBS) // BLOCK).astype(jnp.int32)
    sims_all = evolved.reshape(SIM_BLOCKS, BLOCK, P_SIZE)
    params_all = jnp.transpose(sim_params.reshape(NPARAM, SIM_BLOCKS, BLOCK), (1, 0, 2))
    class_all = sim_class.reshape(SIM_BLOCKS, BLOCK)
    block_ids = jnp.arange(SIM_BLOCKS).astype(jnp.int32)

    def step(carry, inputs):
        sims, params, sims_class, block_id = inputs
        column = lax.dynamic_slice_in_dim(pattern, block_id, 1, 1)[:, 0]
        rows_open = column[row_block] == 1
        result = visit_block(observed, obs_sq, sharpness, obs_class, rows_open, sims, params, sims_class, carry[0], carry[1], carry[2])
        return result, None

    start = (jnp.full((NOBS,), NEG_START, jnp.float32), jnp.zeros((NOBS,), jnp.float32), jnp.zeros((NPARAM, NOBS), jnp.float32))
    final, _ = lax.scan(step, start, (sims_all, params_all, class_all, block_ids))
    running_max, weight_total, param_sums = final
    return param_sums / weight_total[None, :], running_max + jnp.log(weight_total)
```

```python
import functools

import jax
import jax.numpy as jnp
from jax import lax
from jax.experimental import pallas as pl
from jax.experimental.pallas import tpu as pltpu
from jax.sharding import PartitionSpec as P

NEG_START = -1e30
NEG_MASK = -3e38
LANES = 128
AUX_ROWS = 16
MESH = pl.DeviceIdType.MESH


def gather_and_absorb(
    depth,
    obs_hbm,
    sharp_hbm,
    ocls_hbm,
    pat_hbm,
    evo_hbm,
    prm_hbm,
    scls_hbm,
    out_ref,
    gat,
    aux,
    obs,
    sharp_in,
    ocls_in,
    pat_ref,
    prm_ref,
    scls_in,
    stage,
    sharp_ref,
    ocls_ref,
    base_sc,
    max_sc,
    tot_sc,
    sum_sc,
    local_sem,
    up_send,
    dn_send,
    z_recv,
    y_send,
    y_recv,
    s_send,
    s_recv,
):
    me = lax.axis_index("blk")
    z, y, c = me // 4, (me // 2) % 2, me % 2
    rows, feat = obs.shape
    sims = evo_hbm.shape[0]
    half, quarter = sims // 2, sims // 4
    tile_count = pat_hbm.shape[0]
    tile_rows = rows // tile_count
    nparam = prm_hbm.shape[0]

    def blk_of(zz, yy, cc):
        return zz * 4 + yy * 2 + cc

    evo_copy = pltpu.make_async_copy(evo_hbm, gat.at[z, y, c], local_sem.at[0])
    prm_copy = pltpu.make_async_copy(prm_hbm, prm_ref, local_sem.at[1])
    scls_copy = pltpu.make_async_copy(scls_hbm, scls_in, local_sem.at[2])
    obs_copy = pltpu.make_async_copy(obs_hbm, obs, local_sem.at[3])
    sharp_copy = pltpu.make_async_copy(sharp_hbm, sharp_in, local_sem.at[4])
    ocls_copy = pltpu.make_async_copy(ocls_hbm, ocls_in, local_sem.at[5])
    pat_copy = pltpu.make_async_copy(pat_hbm, pat_ref, local_sem.at[6])

    has_up = z < depth - 1
    has_dn = z > 0
    barrier = pltpu.get_barrier_semaphore()

    def greet(dev):
        pl.semaphore_signal(barrier, inc=1, device_id={"blk": dev}, device_id_type=MESH)

    greet(blk_of(z, y, 1 - c))
    greet(blk_of(z, 1 - y, c))

    @pl.when(has_up)
    def _():
        greet(blk_of(z + 1, y, c))

    @pl.when(has_dn)
    def _():
        greet(blk_of(z - 1, y, c))

    for copy in (evo_copy, prm_copy, scls_copy, obs_copy, sharp_copy, ocls_copy, pat_copy):
        copy.start()

    def is_end(o):
        return (o == 0) | (o == depth - 1)

    def remote(src, dst, dev, send, recv):
        return pltpu.make_async_remote_copy(
            src_ref=src,
            dst_ref=dst,
            send_sem=send,
            recv_sem=recv,
            device_id={"blk": dev},
            device_id_type=MESH,
        )

    def part(o, yy, cc, first, count, own):
        dst = gat.at[o, yy, cc, pl.ds(first, count)]
        return (evo_hbm.at[pl.ds(first, count)] if own else dst), dst

    def along_z(o, slot, own, zz, send):
        if slot == 4:
            src = dst = aux.at[o, y, c]
        elif slot >= 2:
            src, dst = part(o, 1 - y, c, (2 * slot - 3) * quarter, quarter, False)
        else:
            src, dst = part(o, y, c, slot * half, half, own)
        k = o * 5 + slot
        return remote(src, dst, blk_of(zz, y, c), send.at[k], z_recv.at[k])

    def to_up(o, slot, own=False):
        return along_z(o, slot, own, z + 1, up_send)

    def to_dn(o, slot, own=False):
        return along_z(o, slot, own, z - 1, dn_send)

    def across_y(o, yy, slot, count, own):
        if slot == 4:
            src = dst = aux.at[o, yy, c]
        else:
            src, dst = part(o, yy, c, slot * quarter, count, own)
        k = o * 5 + slot
        return remote(src, dst, blk_of(z, 1 - y, c), y_send.at[k], y_recv.at[k])

    def to_y(o, slot, count=0, own=False):
        return across_y(o, y, slot, count, own)

    def from_y(o, slot, count=0):
        return across_y(o, 1 - y, slot, count, False)

    def core_hop(o, yy, cc, slot, own):
        if slot == 2:
            src = dst = aux.at[o, yy, cc]
        else:
            src, dst = part(o, yy, cc, slot * half, half, own)
        k = (o * 2 + yy) * 3 + slot
        return remote(src, dst, blk_of(z, y, 1 - c), s_send.at[k], s_recv.at[k])

    def to_core(o, yy, slot, own=False):
        return core_hop(o, yy, c, slot, own)

    def from_core(o, yy, slot):
        return core_hop(o, yy, 1 - c, slot, False)

    def both_ways(o, slot, own):
        @pl.when(has_up)
        def _():
            to_up(o, slot, own).start()

        @pl.when(has_dn)
        def _():
            to_dn(o, slot, own).start()

    peers = 2 + (z + depth - 1) // depth + (2 * depth - 2 - z) // depth
    pl.semaphore_wait(barrier, peers)

    both_ways(z, 0, True)

    @pl.when(is_end(z))
    def _():
        for slot in (1, 3, 0, 2):
            to_y(z, slot, quarter, True).start()

    @pl.when(jnp.logical_not(is_end(z)))
    def _():
        for slot in (0, 2):
            to_y(z, slot, half, True).start()

    both_ways(z, 1, True)
    to_core(z, y, 0, True).start()
    to_core(z, y, 1, True).start()

    stage[...] = jnp.zeros_like(stage)
    prm_copy.wait()
    stage[0:nparam, :] = prm_ref[...].astype(jnp.float32)
    scls_copy.wait()
    stage[nparam : nparam + 1, :] = scls_in[...].reshape(1, sims).astype(jnp.float32)
    evo_copy.wait()
    block = gat[z, y, c].astype(jnp.float32)
    own_sq = 0.5 * jnp.sum(block * block, axis=1, keepdims=True)
    left = jnp.broadcast_to(own_sq, (LANES, LANES)).T[0:1, :]
    for k in range(3):
        piece = left.astype(jnp.bfloat16).astype(jnp.float32)
        stage[nparam + 1 + k : nparam + 2 + k, :] = piece
        left = left - piece
    aux[z, y, c] = stage[...].astype(jnp.bfloat16)
    both_ways(z, 4, True)
    to_y(z, 4).start()
    to_core(z, y, 2).start()

    sharp_copy.wait()
    ocls_copy.wait()
    pat_copy.wait()
    obs_copy.wait()
    for i in range(rows // LANES):
        lanes = slice(i * LANES, (i + 1) * LANES)
        sharp_ref[0:1, lanes] = 2.0 * sharp_in[lanes].reshape(1, LANES)
        ocls_ref[0:1, lanes] = ocls_in[lanes].reshape(1, LANES)
        rows_f32 = obs[i * LANES : (i + 1) * LANES, :].astype(jnp.float32)
        col = jnp.sum(rows_f32 * rows_f32, axis=1, keepdims=True)
        wide = jnp.broadcast_to(col, (LANES, LANES)).T
        base_sc[0:1, lanes] = 1.0 * feat - 0.5 * wide[0:1, :]

    max_sc[...] = jnp.full_like(max_sc, NEG_START)
    tot_sc[...] = jnp.zeros_like(tot_sc)
    sum_sc[...] = jnp.zeros_like(sum_sc)

    def absorb(o, yy, first, count):
        span = slice(first, first + count)
        lhs, half_sq, classes, params = [], [], [], []
        for cc in range(2):
            lhs.append(gat[o, yy, cc, span, :])
            packet = aux[o, yy, cc]
            packet_f32 = packet.astype(jnp.float32)
            row = packet_f32[nparam : nparam + 1, :]
            row_sq = (
                packet_f32[nparam + 1 : nparam + 2, :]
                + packet_f32[nparam + 2 : nparam + 3, :]
                + packet_f32[nparam + 3 : nparam + 4, :]
            )
            classes.append(jnp.broadcast_to(row, (LANES, LANES)).T[span, 0:1])
            half_sq.append(jnp.broadcast_to(row_sq, (LANES, LANES)).T[span, 0:1])
            params.append(packet[:, span])
        product = lax.dot_general(
            jnp.concatenate(lhs, axis=0),
            obs[...],
            (((1,), (1,)), ((), ())),
            preferred_element_type=jnp.float32,
        )
        sharp2 = sharp_ref[...]
        base = base_sc[...]
        masked = []
        for cc in range(2):
            wanted = jnp.concatenate(
                [
                    jnp.where(
                        pat_ref[i, blk_of(o, yy, cc)] == 1,
                        ocls_ref[0:1, i * tile_rows : (i + 1) * tile_rows],
                        -1,
                    )
                    for i in range(tile_count)
                ],
                axis=1,
            ).astype(jnp.float32)
            score = ((product[cc * count : (cc + 1) * count] - half_sq[cc]) + base) * sharp2
            masked.append(jnp.where(classes[cc] == wanted, score, NEG_MASK))
        top = jnp.max(jnp.maximum(masked[0], masked[1]), axis=0, keepdims=True)
        old = max_sc[...]
        new = jnp.maximum(old, top)
        factor = jnp.exp(old - new)
        w0 = jnp.exp(masked[0] - new)
        w1 = jnp.exp(masked[1] - new)
        max_sc[...] = new
        tot_sc[...] = tot_sc[...] * factor + jnp.sum(w0 + w1, axis=0, keepdims=True)
        added = lax.dot_general(
            jnp.concatenate(params, axis=1),
            jnp.concatenate([w0, w1], axis=0).astype(jnp.bfloat16),
            (((1,), (0,)), ((), ())),
            preferred_element_type=jnp.float32,
        )
        sum_sc[...] = sum_sc[...] * factor + added

    def drain(o):
        for slot in (0, 1, 4):

            @pl.when(has_up & (o <= z))
            def _():
                to_up(o, slot).wait_send()

            @pl.when(has_dn & (o >= z))
            def _():
                to_dn(o, slot).wait_send()

        @pl.when(is_end(o))
        def _():
            for slot in (2, 3):

                @pl.when(has_up & (o <= z))
                def _():
                    to_up(o, slot).wait_send()

                @pl.when(has_dn & (o >= z))
                def _():
                    to_dn(o, slot).wait_send()

            for slot in (0, 2):
                to_y(o, slot, quarter).wait_send()

            @pl.when(o == z)
            def _():
                for slot in (1, 3):
                    to_y(o, slot, quarter).wait_send()

        @pl.when(jnp.logical_not(is_end(o)))
        def _():
            for slot in (0, 2):
                to_y(o, slot, half).wait_send()

        to_y(o, 4).wait_send()
        for slot in range(3):
            to_core(o, y, slot).wait_send()
            to_core(o, 1 - y, slot).wait_send()

    def step(s, carry):
        def sides(dist):
            lo, hi = z - dist, z + dist
            return (
                (lo, (lo >= 0) & (dist >= 0), has_up, to_up),
                (hi, (hi < depth) & (dist > 0), has_dn, to_dn),
            )

        def pass_on(o, slot, further, to):
            to(o, slot).wait_recv()

            @pl.when(further)
            def _():
                to(o, slot).start()

        def row_half(k):
            for o, there, further, to in sides(s):

                @pl.when(there)
                def _():
                    pass_on(o, k, further, to)

                    @pl.when(is_end(o))
                    def _():
                        if k == 0:
                            to_y(o, 0, quarter).start()
                        else:
                            to_y(o, 2, quarter).start()

                    @pl.when(jnp.logical_not(is_end(o)))
                    def _():
                        to_y(o, 2 * k, half).start()

                    to_core(o, y, k).start()
                    if k == 1:
                        pass_on(o, 4, further, to)
                        to_y(o, 4).start()
                        to_core(o, y, 2).start()

        def crossing(k):
            for o, there, further, to in sides(s - 1):

                @pl.when(there & is_end(o) & (o != z))
                def _():
                    @pl.when(s < depth)
                    def _():
                        if k == 0:
                            pass_on(o, 2, further, to)
                            pass_on(o, 3, further, to)

                    @pl.when(s == depth)
                    def _():
                        to(o, 2 + k).wait_recv()

        def other_half(k):
            for o, there, further, to in sides(s - 1):

                @pl.when(there & is_end(o) & (o != z))
                def _():
                    from_y(o, 2 * k, quarter).wait_recv()

                @pl.when(there & jnp.logical_not(is_end(o)))
                def _():
                    from_y(o, 2 * k, half).wait_recv()

                @pl.when(there & is_end(o) & (o == z))
                def _():
                    if k == 0:
                        for j in range(2):
                            from_y(o, 1 + 2 * j, quarter).wait_recv()
                            both_ways(o, 2 + j, False)
                        from_y(o, 0, quarter).wait_recv()
                    else:
                        from_y(o, 2, quarter).wait_recv()

                @pl.when(there)
                def _():
                    to_core(o, 1 - y, k).start()
                    if k == 1:
                        from_y(o, 4).wait_recv()
                        to_core(o, 1 - y, 2).start()

        def pick(q, carry_q):
            side, k = q % 2, q // 2
            dist = s - 1 - k
            o = z + (2 * side - 1) * dist
            yy = y + k * (1 - 2 * y)

            @pl.when((o >= 0) & (o < depth) & (dist >= 0) & ((dist > 0) | (side == 0)))
            def _():
                for slot in range(3):
                    from_core(o, yy, slot).wait_recv()
                absorb(o, yy, 0, sims)

            for kk in range(2):

                @pl.when((side == 1) & (k == kk))
                def _():
                    row_half(kk)
                    crossing(kk)
                    other_half(kk)

            return carry_q

        lax.fori_loop(0, 4, pick, 0)

        for o, there, _, _ in sides(s - 2):

            @pl.when(there)
            def _():
                drain(o)

        return carry

    lax.fori_loop(1, depth + 1, step, 0)

    @pl.when(is_end(z))
    def _():
        far = depth - 1 - z
        from_core(far, 1 - y, 2).wait_recv()
        from_core(far, 1 - y, 0).wait_recv()
        absorb(far, 1 - y, 0, half)
        from_core(far, 1 - y, 1).wait_recv()
        absorb(far, 1 - y, half, half)
        drain(far)

    out_ref[0:nparam, :] = sum_sc[0:nparam, :]
    out_ref[nparam : nparam + 1, :] = max_sc[...]
    out_ref[nparam + 1 : nparam + 2, :] = tot_sc[...]


def finish(state, mean_ref, lev_ref):
    nparam, rows = mean_ref.shape
    total = state[nparam + 1 : nparam + 2, :]
    mean_ref[...] = state[0:nparam, :] / total
    lev = state[nparam : nparam + 1, :] + jnp.log(total)
    for i in range(rows // LANES):
        lanes = slice(i * LANES, (i + 1) * LANES)
        lev_ref[lanes] = lev[0:1, lanes].reshape(LANES)


def solution(mesh):
    depth = mesh.shape["blk"] // 4

    def on_device(observed, sharpness, obs_class, pattern, evolved, sim_params, sim_class):
        rows, feat = observed.shape
        sims = evolved.shape[0]
        nparam = sim_params.shape[0]
        vmem = pl.BlockSpec(memory_space=pltpu.VMEM)
        hbm = pl.BlockSpec(memory_space=pltpu.HBM)
        dma = pltpu.SemaphoreType.DMA
        arguments = (observed, sharpness, obs_class, pattern, evolved, sim_params, sim_class)
        state = pl.pallas_call(
            functools.partial(gather_and_absorb, depth),
            out_shape=pltpu.VMEM((8, rows), jnp.float32),
            in_specs=[hbm] * 7,
            out_specs=vmem,
            scratch_shapes=[
                pltpu.VMEM((depth, 2, 2, sims, feat), jnp.bfloat16),
                pltpu.VMEM((depth, 2, 2, AUX_ROWS, LANES), jnp.bfloat16),
                pltpu.VMEM((rows, feat), jnp.bfloat16),
                pltpu.VMEM((rows,), jnp.float32),
                pltpu.VMEM((rows,), jnp.int32),
                pltpu.SMEM(pattern.shape, jnp.int32),
                pltpu.VMEM((nparam, sims), jnp.bfloat16),
                pltpu.VMEM((sims,), jnp.int32),
                pltpu.VMEM((AUX_ROWS, LANES), jnp.float32),
                pltpu.VMEM((1, rows), jnp.float32),
                pltpu.VMEM((1, rows), jnp.int32),
                pltpu.VMEM((1, rows), jnp.float32),
                pltpu.VMEM((1, rows), jnp.float32),
                pltpu.VMEM((1, rows), jnp.float32),
                pltpu.VMEM((AUX_ROWS, rows), jnp.float32),
                dma((7,)),
                dma((5 * depth,)),
                dma((5 * depth,)),
                dma((5 * depth,)),
                dma((5 * depth,)),
                dma((5 * depth,)),
                dma((6 * depth,)),
                dma((6 * depth,)),
            ],
            compiler_params=pltpu.CompilerParams(
                collective_id=0, has_side_effects=True, vmem_limit_bytes=40 << 20
            ),
        )(*(pltpu.with_memory_space_constraint(a, pltpu.HBM) for a in arguments))
        return pl.pallas_call(
            finish,
            out_shape=(
                jax.ShapeDtypeStruct((nparam, rows), jnp.float32),
                jax.ShapeDtypeStruct((rows,), jnp.float32),
            ),
            in_specs=[vmem],
            out_specs=(vmem, vmem),
            compiler_params=pltpu.CompilerParams(vmem_limit_bytes=4 << 20),
        )(pltpu.with_memory_space_constraint(state, pltpu.VMEM))

    placed = (
        P(("parts", "blk"), None),
        P(("parts", "blk")),
        P(("parts", "blk")),
        P(("parts", "blk"), None),
        P(("parts", "blk"), None),
        P(None, ("parts", "blk")),
        P(("parts", "blk")),
    )
    return jax.shard_map(
        on_device,
        mesh=mesh,
        in_specs=placed,
        out_specs=(P(None, ("parts", "blk")), P(("parts", "blk"))),
        check_vma=False,
    )
```

```python
import functools

import jax
import jax.numpy as jnp
from jax import lax
from jax.experimental import pallas as pl
from jax.experimental.pallas import tpu as pltpu
from jax.sharding import PartitionSpec as P

NEG_START = -1e30
NEG_MASK = -3e38
LANES = 128
AUX_ROWS = 16
MESH = pl.DeviceIdType.MESH


def gather_and_absorb(
    depth,
    obs_hbm,
    sharp_hbm,
    ocls_hbm,
    pat_hbm,
    evo_hbm,
    prm_hbm,
    scls_hbm,
    out_ref,
    gat,
    aux,
    obs,
    obs_t,
    sharp_in,
    ocls_in,
    pat_ref,
    prm_ref,
    scls_in,
    stage,
    sharp_ref,
    ocls_ref,
    base_sc,
    max_sc,
    tot_sc,
    sum_sc,
    local_sem,
    up_send,
    dn_send,
    z_recv,
    y_send,
    y_recv,
    s_send,
    s_recv,
    ready,
):
    me = lax.axis_index("blk")
    z, y, c = me // 4, (me // 2) % 2, me % 2
    rows, feat = obs.shape
    sims = evo_hbm.shape[0]
    half, quarter = sims // 2, sims // 4
    tile_count = pat_hbm.shape[0]
    tile_rows = rows // tile_count
    nparam = prm_hbm.shape[0]

    def blk_of(zz, yy, cc):
        return zz * 4 + yy * 2 + cc

    evo_copy = pltpu.make_async_copy(evo_hbm, gat.at[z, y, c], local_sem.at[0])
    prm_copy = pltpu.make_async_copy(prm_hbm, prm_ref, local_sem.at[1])
    scls_copy = pltpu.make_async_copy(scls_hbm, scls_in, local_sem.at[2])
    obs_copy = pltpu.make_async_copy(obs_hbm, obs, local_sem.at[3])
    sharp_copy = pltpu.make_async_copy(sharp_hbm, sharp_in, local_sem.at[4])
    ocls_copy = pltpu.make_async_copy(ocls_hbm, ocls_in, local_sem.at[5])
    pat_copy = pltpu.make_async_copy(pat_hbm, pat_ref, local_sem.at[6])

    has_up = z < depth - 1
    has_dn = z > 0
    barrier = pltpu.get_barrier_semaphore()

    def greet(dev):
        pl.semaphore_signal(barrier, inc=1, device_id={"blk": dev}, device_id_type=MESH)

    @pl.when(has_up)
    def _():
        greet(blk_of(z + 1, y, c))

    @pl.when(y == 0)
    def _():
        greet(blk_of(z, 1, c))

    @pl.when(c == 0)
    def _():
        greet(blk_of(z, y, 1))

    for copy in (evo_copy, prm_copy, scls_copy, obs_copy, sharp_copy, ocls_copy, pat_copy):
        copy.start()

    def is_end(o):
        return (o == 0) | (o == depth - 1)

    def remote(src, dst, dev, send, recv):
        return pltpu.make_async_remote_copy(
            src_ref=src,
            dst_ref=dst,
            send_sem=send,
            recv_sem=recv,
            device_id={"blk": dev},
            device_id_type=MESH,
        )

    def part(o, yy, cc, first, count, own):
        dst = gat.at[o, yy, cc, pl.ds(first, count)]
        return (evo_hbm.at[pl.ds(first, count)] if own else dst), dst

    def along_z(o, slot, own, zz, send):
        if slot == 4:
            src = dst = aux.at[o, y, c]
        elif slot > 4:
            src, dst = part(o, 1 - y, c, (2 * slot - 9) * quarter, quarter, False)
        else:
            src, dst = part(o, y, c, slot * quarter, quarter, own)
        k = o * 7 + slot
        return remote(src, dst, blk_of(zz, y, c), send.at[k], z_recv.at[k])

    def to_up(o, slot, own=False):
        return along_z(o, slot, own, z + 1, up_send)

    def to_dn(o, slot, own=False):
        return along_z(o, slot, own, z - 1, dn_send)

    def across_y(o, yy, slot, own):
        if slot == 4:
            src = dst = aux.at[o, yy, c]
        else:
            src, dst = part(o, yy, c, slot * quarter, quarter, own)
        k = o * 5 + slot
        return remote(src, dst, blk_of(z, 1 - y, c), y_send.at[k], y_recv.at[k])

    def to_y(o, slot, own=False):
        return across_y(o, y, slot, own)

    def from_y(o, slot):
        return across_y(o, 1 - y, slot, False)

    def core_hop(o, yy, cc, slot, own):
        if isinstance(slot, int) and slot == 2:
            src = dst = aux.at[o, yy, cc]
        else:
            src, dst = part(o, yy, cc, slot * half, half, own)
        k = (o * 2 + yy) * 3 + slot
        return remote(src, dst, blk_of(z, y, 1 - c), s_send.at[k], s_recv.at[k])

    def to_core(o, yy, slot, own=False):
        return core_hop(o, yy, c, slot, own)

    def from_core(o, yy, slot):
        return core_hop(o, yy, 1 - c, slot, False)

    def tell(k, dev):
        pl.semaphore_signal(ready.at[k], inc=1, device_id={"blk": dev}, device_id_type=MESH)

    def own_z(to, slots):
        for slot in slots:
            to(z, slot, True).start()

    def own_y(first, last):
        @pl.when(is_end(z))
        def _():
            for slot in (1, 0, 4, 3, 2)[first:last]:
                to_y(z, slot, True).start()

        @pl.when(jnp.logical_not(is_end(z)))
        def _():
            for slot in (0, 1, 4, 2, 3)[first:last]:
                to_y(z, slot, True).start()

    nearer = (z + depth - 1) // depth + y + c

    @pl.when(nearer > 0)
    def _():
        pl.semaphore_wait(barrier, nearer)

    @pl.when(has_dn)
    def _():
        own_z(to_dn, (0, 1))
        tell(0, blk_of(z - 1, y, c))

    @pl.when(y == 1)
    def _():
        own_y(0, 2)
        tell(1, blk_of(z, 0, c))

    @pl.when(c == 1)
    def _():
        tell(2, blk_of(z, y, 0))

    stage[...] = jnp.zeros_like(stage)
    prm_copy.wait()
    stage[0:nparam, :] = prm_ref[...].astype(jnp.float32)
    scls_copy.wait()
    stage[nparam : nparam + 1, :] = scls_in[...].reshape(1, sims).astype(jnp.float32)
    evo_copy.wait()
    block = gat[z, y, c].astype(jnp.float32)
    own_sq = 0.5 * jnp.sum(block * block, axis=1, keepdims=True)
    left = jnp.broadcast_to(own_sq, (LANES, LANES)).T[0:1, :]
    for k in range(3):
        piece = left.astype(jnp.bfloat16).astype(jnp.float32)
        stage[nparam + 1 + k : nparam + 2 + k, :] = piece
        left = left - piece
    aux[z, y, c] = stage[...].astype(jnp.bfloat16)

    @pl.when(has_dn)
    def _():
        own_z(to_dn, (4, 2, 3))

    @pl.when(y == 1)
    def _():
        own_y(2, 5)

    @pl.when(has_up)
    def _():
        pl.semaphore_wait(ready.at[0], 1)
        own_z(to_up, (0, 1, 4, 2, 3))

    @pl.when(y == 0)
    def _():
        pl.semaphore_wait(ready.at[1], 1)
        own_y(0, 5)

    @pl.when(c == 0)
    def _():
        pl.semaphore_wait(ready.at[2], 1)

    for slot in range(3):
        to_core(z, y, slot, True).start()

    sharp_copy.wait()
    ocls_copy.wait()
    pat_copy.wait()
    obs_copy.wait()
    for i in range(rows // LANES):
        lanes = slice(i * LANES, (i + 1) * LANES)
        sharp_ref[0:1, lanes] = 2.0 * sharp_in[lanes].reshape(1, LANES)
        ocls_ref[0:1, lanes] = ocls_in[lanes].reshape(1, LANES)
        turned = obs[lanes, :].T
        obs_t[:, lanes] = turned
        wide = turned.astype(jnp.float32)
        base_sc[0:1, lanes] = 1.0 * feat - 0.5 * jnp.sum(wide * wide, axis=0, keepdims=True)

    max_sc[...] = jnp.full_like(max_sc, NEG_START)
    tot_sc[...] = jnp.zeros_like(tot_sc)
    sum_sc[...] = jnp.zeros_like(sum_sc)

    first_half = lax.broadcasted_iota(jnp.int32, (AUX_ROWS, LANES), 1) < half

    def absorb(parts):
        lhs, half_sq, classes, params = [], [], [], []
        for o, yy, h in parts:
            packets = []
            for cc in range(2):
                lhs.append(gat[o, yy, cc, pl.ds(pl.multiple_of(h * half, half), half), :])
                packet = aux[o, yy, cc].astype(jnp.float32)
                packets.append(jnp.where(h == cc, packet, pltpu.roll(packet, half, 1)))
            packet = jnp.where(first_half, packets[0], packets[1])
            params.append(packet)
            column = packet[0:8, :].T
            classes.append(column[:, nparam : nparam + 1])
            half_sq.append(
                column[:, nparam + 1 : nparam + 2]
                + column[:, nparam + 2 : nparam + 3]
                + column[:, nparam + 3 : nparam + 4]
            )
        product = lax.dot_general(
            jnp.concatenate(lhs, axis=0),
            obs_t[...],
            (((1,), (0,)), ((), ())),
            preferred_element_type=jnp.float32,
        )
        sharp2 = sharp_ref[...]
        base = base_sc[...]
        masked = []
        for p, (o, yy, _) in enumerate(parts):
            for cc in range(2):
                wanted = jnp.concatenate(
                    [
                        jnp.where(
                            pat_ref[i, blk_of(o, yy, cc)] == 1,
                            ocls_ref[0:1, i * tile_rows : (i + 1) * tile_rows],
                            -1,
                        )
                        for i in range(tile_count)
                    ],
                    axis=1,
                ).astype(jnp.float32)
                mine = slice(cc * half, (cc + 1) * half)
                span = slice((2 * p + cc) * half, (2 * p + cc + 1) * half)
                score = ((product[span] - half_sq[p][mine]) + base) * sharp2
                masked.append(jnp.where(classes[p][mine] == wanted, score, NEG_MASK))
        top = functools.reduce(jnp.maximum, masked)
        old = max_sc[...]
        new = jnp.maximum(old, jnp.max(top, axis=0, keepdims=True))
        factor = jnp.exp(old - new)
        weights = [jnp.exp(m - new) for m in masked]
        max_sc[...] = new
        tot_sc[...] = tot_sc[...] * factor + jnp.sum(sum(weights), axis=0, keepdims=True)
        added = lax.dot_general(
            jnp.concatenate(params, axis=1).astype(jnp.bfloat16),
            jnp.concatenate(weights, axis=0).astype(jnp.bfloat16),
            (((1,), (0,)), ((), ())),
            preferred_element_type=jnp.float32,
        )
        sum_sc[...] = sum_sc[...] * factor + added

    def drain_z(o, slot):
        @pl.when(has_up & (o <= z))
        def _():
            to_up(o, slot).wait_send()

        @pl.when(has_dn & (o >= z))
        def _():
            to_dn(o, slot).wait_send()

    def drain(o):
        for slot in range(5):
            drain_z(o, slot)

        @pl.when(is_end(o))
        def _():
            drain_z(o, 5)
            drain_z(o, 6)

        @pl.when(jnp.logical_not(is_end(o)) | (o == z))
        def _():
            to_y(o, 1).wait_send()
            to_y(o, 3).wait_send()

        for slot in (0, 2, 4):
            to_y(o, slot).wait_send()
        for slot in range(3):
            to_core(o, y, slot).wait_send()
            to_core(o, 1 - y, slot).wait_send()

    def sides(dist):
        lo, hi = z - dist, z + dist
        return (
            (lo, (lo >= 0) & (dist >= 0), has_up, to_up),
            (hi, (hi < depth) & (dist > 0), has_dn, to_dn),
        )

    def pass_on(o, slot, further, to):
        to(o, slot).wait_recv()

        @pl.when(further)
        def _():
            to(o, slot).start()

    def same_row(s, q):
        for o, there, further, to in sides(s):

            @pl.when(there)
            def _():
                pass_on(o, q, further, to)
                if q % 2:

                    @pl.when(jnp.logical_not(is_end(o)))
                    def _():
                        to_y(o, q).start()

                    to_core(o, y, q // 2).start()
                else:
                    to_y(o, q).start()
                if q == 1:
                    pass_on(o, 4, further, to)
                    to_y(o, 4).start()
                    to_core(o, y, 2).start()

    def other_row(s, q):
        for o, there, _, to in sides(s - 1):

            @pl.when(there & is_end(o) & (o != z))
            def _():
                if q < 2:
                    from_y(o, 2 * q).wait_recv()
                    if q == 0:
                        from_y(o, 4).wait_recv()
                        to_core(o, 1 - y, 2).start()

                    @pl.when(is_end(z))
                    def _():
                        to(o, 5 + q).wait_recv()

                    to_core(o, 1 - y, q).start()

            @pl.when(there & jnp.logical_not(is_end(o)))
            def _():
                from_y(o, q).wait_recv()
                if q % 2:
                    to_core(o, 1 - y, q // 2).start()
                if q == 1:
                    from_y(o, 4).wait_recv()
                    to_core(o, 1 - y, 2).start()

            @pl.when(there & is_end(o) & (o == z))
            def _():
                from_y(o, (1, 0, 3, 2)[q]).wait_recv()
                if q % 2:
                    to_core(o, 1 - y, q // 2).start()
                else:

                    @pl.when(has_up)
                    def _():
                        to_up(o, 5 + q // 2).start()

                    @pl.when(has_dn)
                    def _():
                        to_dn(o, 5 + q // 2).start()

                if q == 1:
                    from_y(o, 4).wait_recv()
                    to_core(o, 1 - y, 2).start()

    def cross(s, q):
        for o, there, further, to in sides(s):

            @pl.when(there & is_end(o) & (o != z) & further)
            def _():
                to(o, 5 + q).wait_recv()
                to(o, 5 + q).start()

    def settle(dist):
        for o, there, _, _ in sides(dist):

            @pl.when(there)
            def _():
                drain(o)

    def fetch(o, yy, h):
        from_core(o, yy, h).wait_recv()

        @pl.when(h == 0)
        def _():
            from_core(o, yy, 2).wait_recv()

    def turn(i, carry):
        s, q = 1 + i // 4, i % 4
        side, second = q % 2, q // 2
        inner = jnp.where(is_end(z), 0, 1)
        for k in range(4):

            @pl.when(q == k)
            def _():
                if k == 0:
                    settle(s - 3)
                same_row(s, k)
                if k < 2:
                    cross(s - 1, k)

        dist = jnp.where(inner == 1, s - 1, s - 1 + second)
        h = jnp.where(inner == 1, second, 1 - second)
        sign = 2 * side - 1
        row_o, other_o = z + sign * dist, z + sign * (dist - 1)
        opening = (dist == 0) & (q == 0)
        row_ok = (row_o >= 0) & (row_o < depth) & ((dist > 0) | (q == 0))
        near = (dist > 1) | (side == (depth - 1 - z) // (depth - 1))
        other_ok = (other_o >= 0) & (other_o < depth) & (dist > 0) & near

        @pl.when(row_ok & (other_ok | opening))
        def _():
            other_at = jnp.where(opening, z, other_o)
            other_y = jnp.where(opening, y, 1 - y)
            other_h = jnp.where(opening, 1 - h, h)
            fetch(row_o, y, h)
            fetch(other_at, other_y, other_h)
            absorb(((row_o, y, h), (other_at, other_y, other_h)))

        @pl.when((row_ok & jnp.logical_not(other_ok | opening)) | (other_ok & jnp.logical_not(row_ok)))
        def _():
            only_at = jnp.where(row_ok, row_o, other_o)
            only_y = jnp.where(row_ok, y, 1 - y)
            fetch(only_at, only_y, h)
            absorb(((only_at, only_y, h),))

        late = s - inner * (1 - second)
        first = jnp.where(inner == 1, 2 * (1 - second), 2 * second)

        @pl.when((side == 1) & (first == 0))
        def _():
            other_row(late, 0)
            other_row(late, 1)

        @pl.when((side == 1) & (first == 2))
        def _():
            other_row(late, 2)
            other_row(late, 3)

        return carry

    lax.fori_loop(0, 4 * depth + 2, turn, 0)
    settle(depth - 1)

    out_ref[0:nparam, :] = sum_sc[0:nparam, :]
    out_ref[nparam : nparam + 1, :] = max_sc[...]
    out_ref[nparam + 1 : nparam + 2, :] = tot_sc[...]


def finish(state, mean_ref, lev_ref):
    nparam, rows = mean_ref.shape
    total = state[nparam + 1 : nparam + 2, :]
    mean_ref[...] = state[0:nparam, :] / total
    lev = state[nparam : nparam + 1, :] + jnp.log(total)
    for i in range(rows // LANES):
        lanes = slice(i * LANES, (i + 1) * LANES)
        lev_ref[lanes] = lev[0:1, lanes].reshape(LANES)


def solution(mesh):
    depth = mesh.shape["blk"] // 4

    def on_device(observed, sharpness, obs_class, pattern, evolved, sim_params, sim_class):
        rows, feat = observed.shape
        sims = evolved.shape[0]
        nparam = sim_params.shape[0]
        vmem = pl.BlockSpec(memory_space=pltpu.VMEM)
        hbm = pl.BlockSpec(memory_space=pltpu.HBM)
        dma = pltpu.SemaphoreType.DMA
        arguments = (observed, sharpness, obs_class, pattern, evolved, sim_params, sim_class)
        state = pl.pallas_call(
            functools.partial(gather_and_absorb, depth),
            out_shape=pltpu.VMEM((8, rows), jnp.float32),
            in_specs=[hbm] * 7,
            out_specs=vmem,
            scratch_shapes=[
                pltpu.VMEM((depth, 2, 2, sims, feat), jnp.bfloat16),
                pltpu.VMEM((depth, 2, 2, AUX_ROWS, LANES), jnp.bfloat16),
                pltpu.VMEM((rows, feat), jnp.bfloat16),
                pltpu.VMEM((feat, rows), jnp.bfloat16),
                pltpu.VMEM((rows,), jnp.float32),
                pltpu.VMEM((rows,), jnp.int32),
                pltpu.SMEM(pattern.shape, jnp.int32),
                pltpu.VMEM((nparam, sims), jnp.bfloat16),
                pltpu.VMEM((sims,), jnp.int32),
                pltpu.VMEM((AUX_ROWS, LANES), jnp.float32),
                pltpu.VMEM((1, rows), jnp.float32),
                pltpu.VMEM((1, rows), jnp.int32),
                pltpu.VMEM((1, rows), jnp.float32),
                pltpu.VMEM((1, rows), jnp.float32),
                pltpu.VMEM((1, rows), jnp.float32),
                pltpu.VMEM((AUX_ROWS, rows), jnp.float32),
                dma((7,)),
                dma((7 * depth,)),
                dma((7 * depth,)),
                dma((7 * depth,)),
                dma((5 * depth,)),
                dma((5 * depth,)),
                dma((6 * depth,)),
                dma((6 * depth,)),
                pltpu.SemaphoreType.REGULAR((3,)),
            ],
            compiler_params=pltpu.CompilerParams(
                collective_id=0, has_side_effects=True, vmem_limit_bytes=40 << 20
            ),
        )(*(pltpu.with_memory_space_constraint(a, pltpu.HBM) for a in arguments))
        return pl.pallas_call(
            finish,
            out_shape=(
                jax.ShapeDtypeStruct((nparam, rows), jnp.float32),
                jax.ShapeDtypeStruct((rows,), jnp.float32),
            ),
            in_specs=[vmem],
            out_specs=(vmem, vmem),
            compiler_params=pltpu.CompilerParams(vmem_limit_bytes=4 << 20),
        )(pltpu.with_memory_space_constraint(state, pltpu.VMEM))

    placed = (
        P(("parts", "blk"), None),
        P(("parts", "blk")),
        P(("parts", "blk")),
        P(("parts", "blk"), None),
        P(("parts", "blk"), None),
        P(None, ("parts", "blk")),
        P(("parts", "blk")),
    )
    return jax.shard_map(
        on_device,
        mesh=mesh,
        in_specs=placed,
        out_specs=(P(None, ("parts", "blk")), P(("parts", "blk"))),
        check_vma=False,
    )
```

```python
import functools

import jax
import jax.numpy as jnp
from jax import lax
from jax.experimental import pallas as pl
from jax.experimental.pallas import tpu as pltpu
from jax.sharding import PartitionSpec as P

NEG_START = -1e30
NEG_MASK = -3e38
LANES = 128
AUX_ROWS = 16
MESH = pl.DeviceIdType.MESH


def gather_and_absorb(
    depth,
    obs_hbm,
    sharp_hbm,
    ocls_hbm,
    pat_hbm,
    evo_hbm,
    prm_hbm,
    scls_hbm,
    out_ref,
    gat,
    aux,
    obs,
    obs_t,
    sharp_in,
    ocls_in,
    pat_ref,
    prm_ref,
    scls_in,
    stage,
    sharp_ref,
    ocls_ref,
    base_sc,
    max_sc,
    tot_sc,
    sum_sc,
    local_sem,
    up_send,
    dn_send,
    z_recv,
    y_send,
    y_recv,
    s_send,
    s_recv,
    ready,
):
    me = lax.axis_index("blk")
    z, y, c = me // 4, (me // 2) % 2, me % 2
    rows, feat = obs.shape
    sims = evo_hbm.shape[0]
    half, quarter = sims // 2, sims // 4
    tile_count = pat_hbm.shape[0]
    tile_rows = rows // tile_count
    nparam = prm_hbm.shape[0]

    def blk_of(zz, yy, cc):
        return zz * 4 + yy * 2 + cc

    evo_copy = pltpu.make_async_copy(evo_hbm, gat.at[z, y, c], local_sem.at[0])
    prm_copy = pltpu.make_async_copy(prm_hbm, prm_ref, local_sem.at[1])
    scls_copy = pltpu.make_async_copy(scls_hbm, scls_in, local_sem.at[2])
    obs_copy = pltpu.make_async_copy(obs_hbm, obs, local_sem.at[3])
    sharp_copy = pltpu.make_async_copy(sharp_hbm, sharp_in, local_sem.at[4])
    ocls_copy = pltpu.make_async_copy(ocls_hbm, ocls_in, local_sem.at[5])
    pat_copy = pltpu.make_async_copy(pat_hbm, pat_ref, local_sem.at[6])

    has_up = z < depth - 1
    has_dn = z > 0
    barrier = pltpu.get_barrier_semaphore()

    def greet(dev):
        pl.semaphore_signal(barrier, inc=1, device_id={"blk": dev}, device_id_type=MESH)

    @pl.when(has_up)
    def _():
        greet(blk_of(z + 1, y, c))

    @pl.when(y == 0)
    def _():
        greet(blk_of(z, 1, c))

    @pl.when(c == 0)
    def _():
        greet(blk_of(z, y, 1))

    for copy in (evo_copy, prm_copy, scls_copy, obs_copy, sharp_copy, ocls_copy, pat_copy):
        copy.start()

    def is_end(o):
        return (o == 0) | (o == depth - 1)

    def remote(src, dst, dev, send, recv):
        return pltpu.make_async_remote_copy(
            src_ref=src,
            dst_ref=dst,
            send_sem=send,
            recv_sem=recv,
            device_id={"blk": dev},
            device_id_type=MESH,
        )

    def part(o, yy, cc, first, count, own):
        dst = gat.at[o, yy, cc, pl.ds(first, count)]
        return (evo_hbm.at[pl.ds(first, count)] if own else dst), dst

    def along_z(o, slot, own, zz, send):
        if slot == 4:
            src = dst = aux.at[o, y, c]
        elif slot > 4:
            src, dst = part(o, 1 - y, c, (2 * slot - 9) * quarter, quarter, False)
        else:
            src, dst = part(o, y, c, slot * quarter, quarter, own)
        k = o * 7 + slot
        return remote(src, dst, blk_of(zz, y, c), send.at[k], z_recv.at[k])

    def to_up(o, slot, own=False):
        return along_z(o, slot, own, z + 1, up_send)

    def to_dn(o, slot, own=False):
        return along_z(o, slot, own, z - 1, dn_send)

    def across_y(o, yy, slot, own):
        if slot == 4:
            src = dst = aux.at[o, yy, c]
        else:
            src, dst = part(o, yy, c, slot * quarter, quarter, own)
        k = o * 5 + slot
        return remote(src, dst, blk_of(z, 1 - y, c), y_send.at[k], y_recv.at[k])

    def to_y(o, slot, own=False):
        return across_y(o, y, slot, own)

    def from_y(o, slot):
        return across_y(o, 1 - y, slot, False)

    def core_hop(o, yy, cc, slot, own):
        if isinstance(slot, int) and slot == 2:
            src = dst = aux.at[o, yy, cc]
        else:
            src, dst = part(o, yy, cc, slot * half, half, own)
        k = (o * 2 + yy) * 3 + slot
        return remote(src, dst, blk_of(z, y, 1 - c), s_send.at[k], s_recv.at[k])

    def to_core(o, yy, slot, own=False):
        return core_hop(o, yy, c, slot, own)

    def from_core(o, yy, slot):
        return core_hop(o, yy, 1 - c, slot, False)

    def tell(k, dev):
        pl.semaphore_signal(ready.at[k], inc=1, device_id={"blk": dev}, device_id_type=MESH)

    def own_z(to, slots):
        for slot in slots:
            to(z, slot, True).start()

    def own_y(first, last):
        @pl.when(is_end(z))
        def _():
            for slot in (1, 0, 4, 3, 2)[first:last]:
                to_y(z, slot, True).start()

        @pl.when(jnp.logical_not(is_end(z)))
        def _():
            for slot in (0, 1, 4, 2, 3)[first:last]:
                to_y(z, slot, True).start()

    nearer = (z + depth - 1) // depth + y + c

    @pl.when(nearer > 0)
    def _():
        pl.semaphore_wait(barrier, nearer)

    @pl.when(has_dn)
    def _():
        own_z(to_dn, (0, 1))
        tell(0, blk_of(z - 1, y, c))

    @pl.when(y == 1)
    def _():
        own_y(0, 2)
        tell(1, blk_of(z, 0, c))

    @pl.when(c == 1)
    def _():
        tell(2, blk_of(z, y, 0))

    stage[...] = jnp.zeros_like(stage)
    prm_copy.wait()
    stage[0:nparam, :] = prm_ref[...].astype(jnp.float32)
    scls_copy.wait()
    stage[nparam : nparam + 1, :] = scls_in[...].reshape(1, sims).astype(jnp.float32)
    evo_copy.wait()
    block = gat[z, y, c].astype(jnp.float32)
    own_sq = 0.5 * jnp.sum(block * block, axis=1, keepdims=True)
    left = jnp.broadcast_to(own_sq, (LANES, LANES)).T[0:1, :]
    for k in range(3):
        piece = left.astype(jnp.bfloat16).astype(jnp.float32)
        stage[nparam + 1 + k : nparam + 2 + k, :] = piece
        left = left - piece
    aux[z, y, c] = stage[...].astype(jnp.bfloat16)

    @pl.when(has_dn)
    def _():
        own_z(to_dn, (4, 2, 3))

    @pl.when(y == 1)
    def _():
        own_y(2, 5)

    @pl.when(has_up)
    def _():
        pl.semaphore_wait(ready.at[0], 1)
        own_z(to_up, (0, 1, 4, 2, 3))

    @pl.when(y == 0)
    def _():
        pl.semaphore_wait(ready.at[1], 1)
        own_y(0, 5)

    @pl.when(c == 0)
    def _():
        pl.semaphore_wait(ready.at[2], 1)

    for slot in range(3):
        to_core(z, y, slot, True).start()

    sharp_copy.wait()
    ocls_copy.wait()
    pat_copy.wait()
    obs_copy.wait()
    for i in range(rows // LANES):
        lanes = slice(i * LANES, (i + 1) * LANES)
        sharp_ref[0:1, lanes] = 2.0 * sharp_in[lanes].reshape(1, LANES)
        ocls_ref[0:1, lanes] = ocls_in[lanes].reshape(1, LANES)
        turned = obs[lanes, :].T
        obs_t[:, lanes] = turned
        wide = turned.astype(jnp.float32)
        base_sc[0:1, lanes] = 1.0 * feat - 0.5 * jnp.sum(wide * wide, axis=0, keepdims=True)

    max_sc[...] = jnp.full_like(max_sc, NEG_START)
    tot_sc[...] = jnp.zeros_like(tot_sc)
    sum_sc[...] = jnp.zeros_like(sum_sc)

    first_half = lax.broadcasted_iota(jnp.int32, (AUX_ROWS, LANES), 1) < half

    def halves(o, yy, h):
        rows_in, packets = [], []
        for cc in range(2):
            rows_in.append(gat[o, yy, cc, pl.ds(pl.multiple_of(h * half, half), half), :])
            packet = aux[o, yy, cc].astype(jnp.float32)
            packets.append(jnp.where(h == cc, packet, pltpu.roll(packet, half, 1)))
        sources = [(blk_of(o, yy, cc), half) for cc in range(2)]
        return rows_in, jnp.where(first_half, packets[0], packets[1]), sources

    def whole(o, yy, cc):
        return [gat[o, yy, cc]], aux[o, yy, cc].astype(jnp.float32), [(blk_of(o, yy, cc), sims)]

    def absorb(*parts):
        lhs, half_sq, classes, params = [], [], [], []
        for rows_in, packet, _ in parts:
            lhs.extend(rows_in)
            params.append(packet)
            column = packet[0:8, :].T
            classes.append(column[:, nparam : nparam + 1])
            half_sq.append(
                column[:, nparam + 1 : nparam + 2]
                + column[:, nparam + 2 : nparam + 3]
                + column[:, nparam + 3 : nparam + 4]
            )
        product = lax.dot_general(
            jnp.concatenate(lhs, axis=0),
            obs_t[...],
            (((1,), (0,)), ((), ())),
            preferred_element_type=jnp.float32,
        )
        sharp2 = sharp_ref[...]
        base = base_sc[...]
        masked = []
        for p, (_, _, sources) in enumerate(parts):
            row = 0
            for source, count in sources:
                wanted = jnp.concatenate(
                    [
                        jnp.where(
                            pat_ref[i, source] == 1,
                            ocls_ref[0:1, i * tile_rows : (i + 1) * tile_rows],
                            -1,
                        )
                        for i in range(tile_count)
                    ],
                    axis=1,
                ).astype(jnp.float32)
                mine = slice(row, row + count)
                span = slice(p * sims + row, p * sims + row + count)
                score = ((product[span] - half_sq[p][mine]) + base) * sharp2
                masked.append(jnp.where(classes[p][mine] == wanted, score, NEG_MASK))
                row += count
        top = functools.reduce(jnp.maximum, masked)
        old = max_sc[...]
        new = jnp.maximum(old, jnp.max(top, axis=0, keepdims=True))
        factor = jnp.exp(old - new)
        weights = [jnp.exp(m - new) for m in masked]
        max_sc[...] = new
        tot_sc[...] = tot_sc[...] * factor + jnp.sum(sum(weights), axis=0, keepdims=True)
        added = lax.dot_general(
            jnp.concatenate(params, axis=1).astype(jnp.bfloat16),
            jnp.concatenate(weights, axis=0).astype(jnp.bfloat16),
            (((1,), (0,)), ((), ())),
            preferred_element_type=jnp.float32,
        )
        sum_sc[...] = sum_sc[...] * factor + added

    def drain_z(o, slot):
        @pl.when(has_up & (o <= z))
        def _():
            to_up(o, slot).wait_send()

        @pl.when(has_dn & (o >= z))
        def _():
            to_dn(o, slot).wait_send()

    def drain(o):
        for slot in range(5):
            drain_z(o, slot)

        @pl.when(is_end(o))
        def _():
            drain_z(o, 5)
            drain_z(o, 6)

        @pl.when(jnp.logical_not(is_end(o)) | (o == z))
        def _():
            to_y(o, 1).wait_send()
            to_y(o, 3).wait_send()

        for slot in (0, 2, 4):
            to_y(o, slot).wait_send()
        for slot in range(3):
            to_core(o, y, slot).wait_send()
            to_core(o, 1 - y, slot).wait_send()

    def sides(dist):
        lo, hi = z - dist, z + dist
        return (
            (lo, (lo >= 0) & (dist >= 0), has_up, to_up),
            (hi, (hi < depth) & (dist > 0), has_dn, to_dn),
        )

    def pass_on(o, slot, further, to):
        to(o, slot).wait_recv()

        @pl.when(further)
        def _():
            to(o, slot).start()

    def same_row(s, q):
        for o, there, further, to in sides(s):

            @pl.when(there)
            def _():
                pass_on(o, q, further, to)
                if q % 2:

                    @pl.when(jnp.logical_not(is_end(o)))
                    def _():
                        to_y(o, q).start()

                    to_core(o, y, q // 2).start()
                else:
                    to_y(o, q).start()
                if q == 1:
                    pass_on(o, 4, further, to)
                    to_y(o, 4).start()
                    to_core(o, y, 2).start()

    def other_row(s, q):
        for o, there, _, to in sides(s - 1):

            @pl.when(there & is_end(o) & (o != z))
            def _():
                if q < 2:
                    from_y(o, 2 * q).wait_recv()
                    if q == 0:
                        from_y(o, 4).wait_recv()
                        to_core(o, 1 - y, 2).start()

                    @pl.when(is_end(z))
                    def _():
                        to(o, 5 + q).wait_recv()

                    to_core(o, 1 - y, q).start()

            @pl.when(there & jnp.logical_not(is_end(o)))
            def _():
                from_y(o, q).wait_recv()
                if q % 2:
                    to_core(o, 1 - y, q // 2).start()
                if q == 1:
                    from_y(o, 4).wait_recv()
                    to_core(o, 1 - y, 2).start()

            @pl.when(there & is_end(o) & (o == z))
            def _():
                from_y(o, (1, 0, 3, 2)[q]).wait_recv()
                if q % 2:
                    to_core(o, 1 - y, q // 2).start()
                else:

                    @pl.when(has_up)
                    def _():
                        to_up(o, 5 + q // 2).start()

                    @pl.when(has_dn)
                    def _():
                        to_dn(o, 5 + q // 2).start()

                if q == 1:
                    from_y(o, 4).wait_recv()
                    to_core(o, 1 - y, 2).start()

    def cross(s, q):
        for o, there, further, to in sides(s):

            @pl.when(there & is_end(o) & (o != z) & further)
            def _():
                to(o, 5 + q).wait_recv()
                to(o, 5 + q).start()

    def settle(dist):
        for o, there, _, _ in sides(dist):

            @pl.when(there)
            def _():
                drain(o)

    def fetch(o, yy, h):
        from_core(o, yy, h).wait_recv()

        @pl.when(h == 0)
        def _():
            from_core(o, yy, 2).wait_recv()

    def turn(i, carry):
        s, q = 1 + i // 4, i % 4
        side, second = q % 2, q // 2
        inner = jnp.where(is_end(z), 0, 1)
        for k in range(4):

            @pl.when(q == k)
            def _():
                if k == 0:
                    settle(s - 3)
                same_row(s, k)
                if k < 2:
                    cross(s - 1, k)

        dist = jnp.where(inner == 1, s - 1, s - 1 + second)
        h = jnp.where(inner == 1, second, 1 - second)
        sign = 2 * side - 1
        row_o, other_o = z + sign * dist, z + sign * (dist - 1)
        opening = (dist == 0) & (q == 0)
        row_ok = (row_o >= 0) & (row_o < depth) & ((dist > 0) | (q == 0))
        near = (dist > 1) | (side == (depth - 1 - z) // (depth - 1))
        other_ok = (other_o >= 0) & (other_o < depth) & (dist > 0) & near

        @pl.when(row_ok & (other_ok | opening))
        def _():
            other_at = jnp.where(opening, z, other_o)
            other_y = jnp.where(opening, y, 1 - y)
            other_h = jnp.where(opening, 1 - h, h)
            fetch(row_o, y, h)
            fetch(other_at, other_y, other_h)
            absorb(halves(row_o, y, h), halves(other_at, other_y, other_h))

        closing = (dist == depth) & is_end(z)

        @pl.when(
            (row_ok & jnp.logical_not(other_ok | opening))
            | (other_ok & jnp.logical_not(row_ok | closing))
        )
        def _():
            only_at = jnp.where(row_ok, row_o, other_o)
            only_y = jnp.where(row_ok, y, 1 - y)
            fetch(only_at, only_y, h)
            absorb(halves(only_at, only_y, h))

        late = s - inner * (1 - second)
        first = jnp.where(inner == 1, 2 * (1 - second), 2 * second)

        @pl.when((side == 1) & (first == 0))
        def _():
            other_row(late, 0)
            other_row(late, 1)

        @pl.when((side == 1) & (first == 2))
        def _():
            other_row(late, 2)
            other_row(late, 3)

        return carry

    lax.fori_loop(0, 4 * depth, turn, 0)

    @pl.when(is_end(z))
    def _():
        far = depth - 1 - z

        def close(k, carry):
            @pl.when(k == 1)
            def _():
                for slot in range(3):
                    from_core(far, 1 - y, slot).wait_recv()

            absorb(whole(far, 1 - y, c + k * (1 - 2 * c)))
            return carry

        lax.fori_loop(0, 2, close, 0)

    settle(depth - 2)
    settle(depth - 1)

    out_ref[0:nparam, :] = sum_sc[0:nparam, :]
    out_ref[nparam : nparam + 1, :] = max_sc[...]
    out_ref[nparam + 1 : nparam + 2, :] = tot_sc[...]


def finish(state, mean_ref, lev_ref):
    nparam, rows = mean_ref.shape
    total = state[nparam + 1 : nparam + 2, :]
    mean_ref[...] = state[0:nparam, :] / total
    lev = state[nparam : nparam + 1, :] + jnp.log(total)
    for i in range(rows // LANES):
        lanes = slice(i * LANES, (i + 1) * LANES)
        lev_ref[lanes] = lev[0:1, lanes].reshape(LANES)


def solution(mesh):
    depth = mesh.shape["blk"] // 4

    def on_device(observed, sharpness, obs_class, pattern, evolved, sim_params, sim_class):
        rows, feat = observed.shape
        sims = evolved.shape[0]
        nparam = sim_params.shape[0]
        vmem = pl.BlockSpec(memory_space=pltpu.VMEM)
        hbm = pl.BlockSpec(memory_space=pltpu.HBM)
        dma = pltpu.SemaphoreType.DMA
        arguments = (observed, sharpness, obs_class, pattern, evolved, sim_params, sim_class)
        state = pl.pallas_call(
            functools.partial(gather_and_absorb, depth),
            out_shape=pltpu.VMEM((8, rows), jnp.float32),
            in_specs=[hbm] * 7,
            out_specs=vmem,
            scratch_shapes=[
                pltpu.VMEM((depth, 2, 2, sims, feat), jnp.bfloat16),
                pltpu.VMEM((depth, 2, 2, AUX_ROWS, LANES), jnp.bfloat16),
                pltpu.VMEM((rows, feat), jnp.bfloat16),
                pltpu.VMEM((feat, rows), jnp.bfloat16),
                pltpu.VMEM((rows,), jnp.float32),
                pltpu.VMEM((rows,), jnp.int32),
                pltpu.SMEM(pattern.shape, jnp.int32),
                pltpu.VMEM((nparam, sims), jnp.bfloat16),
                pltpu.VMEM((sims,), jnp.int32),
                pltpu.VMEM((AUX_ROWS, LANES), jnp.float32),
                pltpu.VMEM((1, rows), jnp.float32),
                pltpu.VMEM((1, rows), jnp.int32),
                pltpu.VMEM((1, rows), jnp.float32),
                pltpu.VMEM((1, rows), jnp.float32),
                pltpu.VMEM((1, rows), jnp.float32),
                pltpu.VMEM((AUX_ROWS, rows), jnp.float32),
                dma((7,)),
                dma((7 * depth,)),
                dma((7 * depth,)),
                dma((7 * depth,)),
                dma((5 * depth,)),
                dma((5 * depth,)),
                dma((6 * depth,)),
                dma((6 * depth,)),
                pltpu.SemaphoreType.REGULAR((3,)),
            ],
            compiler_params=pltpu.CompilerParams(
                collective_id=0, has_side_effects=True, vmem_limit_bytes=40 << 20
            ),
        )(*(pltpu.with_memory_space_constraint(a, pltpu.HBM) for a in arguments))
        return pl.pallas_call(
            finish,
            out_shape=(
                jax.ShapeDtypeStruct((nparam, rows), jnp.float32),
                jax.ShapeDtypeStruct((rows,), jnp.float32),
            ),
            in_specs=[vmem],
            out_specs=(vmem, vmem),
            compiler_params=pltpu.CompilerParams(vmem_limit_bytes=4 << 20),
        )(pltpu.with_memory_space_constraint(state, pltpu.VMEM))

    placed = (
        P(("parts", "blk"), None),
        P(("parts", "blk")),
        P(("parts", "blk")),
        P(("parts", "blk"), None),
        P(("parts", "blk"), None),
        P(None, ("parts", "blk")),
        P(("parts", "blk")),
    )
    return jax.shard_map(
        on_device,
        mesh=mesh,
        in_specs=placed,
        out_specs=(P(None, ("parts", "blk")), P(("parts", "blk"))),
        check_vma=False,
    )
```

```python
import functools

import jax
import jax.numpy as jnp
from jax import lax
from jax.experimental import pallas as pl
from jax.experimental.pallas import tpu as pltpu
from jax.sharding import PartitionSpec as P

NEG_START = -1e30
NEG_MASK = -3e38
LANES = 128
AUX_ROWS = 16
MESH = pl.DeviceIdType.MESH


def gather_and_absorb(
    depth,
    obs_hbm,
    sharp_hbm,
    ocls_hbm,
    pat_hbm,
    evo_hbm,
    prm_hbm,
    scls_hbm,
    out_ref,
    gat,
    aux,
    obs,
    obs_t,
    sharp_in,
    ocls_in,
    pat_ref,
    prm_ref,
    scls_in,
    stage,
    sharp_ref,
    ocls_ref,
    base_sc,
    max_sc,
    tot_sc,
    sum_sc,
    local_sem,
    up_send,
    dn_send,
    z_recv,
    y_send,
    y_recv,
    s_send,
    s_recv,
    ready,
):
    me = lax.axis_index("blk")
    z, y, c = me // 4, (me // 2) % 2, me % 2
    rows, feat = obs.shape
    sims = evo_hbm.shape[0]
    half, quarter = sims // 2, sims // 4
    tile_count = pat_hbm.shape[0]
    tile_rows = rows // tile_count
    nparam = prm_hbm.shape[0]

    def blk_of(zz, yy, cc):
        return zz * 4 + yy * 2 + cc

    evo_copy = pltpu.make_async_copy(evo_hbm, gat.at[z, y, c], local_sem.at[0])
    prm_copy = pltpu.make_async_copy(prm_hbm, prm_ref, local_sem.at[1])
    scls_copy = pltpu.make_async_copy(scls_hbm, scls_in, local_sem.at[2])
    obs_copy = pltpu.make_async_copy(obs_hbm, obs, local_sem.at[3])
    sharp_copy = pltpu.make_async_copy(sharp_hbm, sharp_in, local_sem.at[4])
    ocls_copy = pltpu.make_async_copy(ocls_hbm, ocls_in, local_sem.at[5])
    pat_copy = pltpu.make_async_copy(pat_hbm, pat_ref, local_sem.at[6])

    has_up = z < depth - 1
    has_dn = z > 0
    barrier = pltpu.get_barrier_semaphore()

    def greet(dev):
        pl.semaphore_signal(barrier, inc=1, device_id={"blk": dev}, device_id_type=MESH)

    @pl.when(has_up)
    def _():
        greet(blk_of(z + 1, y, c))

    @pl.when(y == 0)
    def _():
        greet(blk_of(z, 1, c))

    @pl.when(c == 0)
    def _():
        greet(blk_of(z, y, 1))

    for copy in (evo_copy, prm_copy, scls_copy, obs_copy, sharp_copy, ocls_copy, pat_copy):
        copy.start()

    def is_end(o):
        return (o == 0) | (o == depth - 1)

    def remote(src, dst, dev, send, recv):
        return pltpu.make_async_remote_copy(
            src_ref=src,
            dst_ref=dst,
            send_sem=send,
            recv_sem=recv,
            device_id={"blk": dev},
            device_id_type=MESH,
        )

    def part(o, yy, cc, first, count, own):
        dst = gat.at[o, yy, cc, pl.ds(first, count)]
        return (evo_hbm.at[pl.ds(first, count)] if own else dst), dst

    def along_z(o, slot, own, zz, send):
        if slot == 4:
            src = dst = aux.at[o, y, c]
        elif slot > 4:
            src, dst = part(o, 1 - y, c, (2 * slot - 9) * quarter, quarter, False)
        else:
            src, dst = part(o, y, c, slot * quarter, quarter, own)
        k = o * 7 + slot
        return remote(src, dst, blk_of(zz, y, c), send.at[k], z_recv.at[k])

    def to_up(o, slot, own=False):
        return along_z(o, slot, own, z + 1, up_send)

    def to_dn(o, slot, own=False):
        return along_z(o, slot, own, z - 1, dn_send)

    def across_y(o, yy, slot, own):
        if slot == 4:
            src = dst = aux.at[o, yy, c]
        else:
            src, dst = part(o, yy, c, slot * quarter, quarter, own)
        k = o * 5 + slot
        return remote(src, dst, blk_of(z, 1 - y, c), y_send.at[k], y_recv.at[k])

    def to_y(o, slot, own=False):
        return across_y(o, y, slot, own)

    def from_y(o, slot):
        return across_y(o, 1 - y, slot, False)

    def core_hop(o, yy, cc, slot, own):
        if isinstance(slot, int) and slot == 2:
            src = dst = aux.at[o, yy, cc]
        else:
            src, dst = part(o, yy, cc, slot * half, half, own)
        k = (o * 2 + yy) * 3 + slot
        return remote(src, dst, blk_of(z, y, 1 - c), s_send.at[k], s_recv.at[k])

    def to_core(o, yy, slot, own=False):
        return core_hop(o, yy, c, slot, own)

    def from_core(o, yy, slot):
        return core_hop(o, yy, 1 - c, slot, False)

    def tell(k, dev):
        pl.semaphore_signal(ready.at[k], inc=1, device_id={"blk": dev}, device_id_type=MESH)

    def own_z(to, slots):
        for slot in slots:
            to(z, slot, True).start()

    def own_y(first, last):
        @pl.when(is_end(z))
        def _():
            for slot in (1, 0, 4, 3, 2)[first:last]:
                to_y(z, slot, True).start()

        @pl.when(jnp.logical_not(is_end(z)))
        def _():
            for slot in (0, 1, 4, 2, 3)[first:last]:
                to_y(z, slot, True).start()

    nearer = (z + depth - 1) // depth + y + c

    @pl.when(nearer > 0)
    def _():
        pl.semaphore_wait(barrier, nearer)

    @pl.when(has_dn)
    def _():
        own_z(to_dn, (0, 1))
        tell(0, blk_of(z - 1, y, c))

    @pl.when(y == 1)
    def _():
        own_y(0, 2)
        tell(1, blk_of(z, 0, c))

    @pl.when(c == 1)
    def _():
        tell(2, blk_of(z, y, 0))

    stage[...] = jnp.zeros_like(stage)
    prm_copy.wait()
    stage[0:nparam, :] = prm_ref[...].astype(jnp.float32)
    scls_copy.wait()
    stage[nparam : nparam + 1, :] = scls_in[...].reshape(1, sims).astype(jnp.float32)
    evo_copy.wait()
    block = gat[z, y, c].astype(jnp.float32)
    own_sq = 0.5 * jnp.sum(block * block, axis=1, keepdims=True)
    left = jnp.broadcast_to(own_sq, (LANES, LANES)).T[0:1, :]
    for k in range(3):
        piece = left.astype(jnp.bfloat16).astype(jnp.float32)
        stage[nparam + 1 + k : nparam + 2 + k, :] = piece
        left = left - piece
    aux[z, y, c] = stage[...].astype(jnp.bfloat16)

    @pl.when(has_dn)
    def _():
        own_z(to_dn, (4, 2, 3))

    @pl.when(y == 1)
    def _():
        own_y(2, 5)

    @pl.when(has_up)
    def _():
        pl.semaphore_wait(ready.at[0], 1)
        own_z(to_up, (0, 1, 4, 2, 3))

    @pl.when(y == 0)
    def _():
        pl.semaphore_wait(ready.at[1], 1)
        own_y(0, 5)

    @pl.when(c == 0)
    def _():
        pl.semaphore_wait(ready.at[2], 1)

    for slot in range(3):
        to_core(z, y, slot, True).start()

    sharp_copy.wait()
    ocls_copy.wait()
    pat_copy.wait()
    obs_copy.wait()
    for i in range(rows // LANES):
        lanes = slice(i * LANES, (i + 1) * LANES)
        sharp_ref[0:1, lanes] = 2.0 * sharp_in[lanes].reshape(1, LANES)
        ocls_ref[0:1, lanes] = ocls_in[lanes].reshape(1, LANES)
        turned = obs[lanes, :].T
        obs_t[:, lanes] = turned
        wide = turned.astype(jnp.float32)
        base_sc[0:1, lanes] = 1.0 * feat - 0.5 * jnp.sum(wide * wide, axis=0, keepdims=True)

    max_sc[...] = jnp.full_like(max_sc, NEG_START)
    tot_sc[...] = jnp.zeros_like(tot_sc)
    sum_sc[...] = jnp.zeros_like(sum_sc)

    first_half = lax.broadcasted_iota(jnp.int32, (AUX_ROWS, LANES), 1) < half

    def halves(o, yy, h):
        rows_in, packets = [], []
        for cc in range(2):
            rows_in.append(gat[o, yy, cc, pl.ds(pl.multiple_of(h * half, half), half), :])
            packet = aux[o, yy, cc].astype(jnp.float32)
            packets.append(jnp.where(h == cc, packet, pltpu.roll(packet, half, 1)))
        sources = [(blk_of(o, yy, cc), half) for cc in range(2)]
        return rows_in, jnp.where(first_half, packets[0], packets[1]), sources

    def whole(o, yy, cc):
        return [gat[o, yy, cc]], aux[o, yy, cc].astype(jnp.float32), [(blk_of(o, yy, cc), sims)]

    def absorb(*parts):
        lhs, half_sq, classes, params = [], [], [], []
        for rows_in, packet, _ in parts:
            lhs.extend(rows_in)
            params.append(packet)
            column = packet[0:8, :].T
            classes.append(column[:, nparam : nparam + 1])
            half_sq.append(
                column[:, nparam + 1 : nparam + 2]
                + column[:, nparam + 2 : nparam + 3]
                + column[:, nparam + 3 : nparam + 4]
            )
        product = lax.dot_general(
            jnp.concatenate(lhs, axis=0),
            obs_t[...],
            (((1,), (0,)), ((), ())),
            preferred_element_type=jnp.float32,
        )
        sharp2 = sharp_ref[...]
        base = base_sc[...]
        masked = []
        for p, (_, _, sources) in enumerate(parts):
            row = 0
            for source, count in sources:
                wanted = jnp.concatenate(
                    [
                        jnp.where(
                            pat_ref[i, source] == 1,
                            ocls_ref[0:1, i * tile_rows : (i + 1) * tile_rows],
                            -1,
                        )
                        for i in range(tile_count)
                    ],
                    axis=1,
                ).astype(jnp.float32)
                mine = slice(row, row + count)
                span = slice(p * sims + row, p * sims + row + count)
                score = ((product[span] - half_sq[p][mine]) + base) * sharp2
                masked.append(jnp.where(classes[p][mine] == wanted, score, NEG_MASK))
                row += count
        top = functools.reduce(jnp.maximum, masked)
        old = max_sc[...]
        new = jnp.maximum(old, jnp.max(top, axis=0, keepdims=True))
        factor = jnp.exp(old - new)
        weights = [jnp.exp(m - new) for m in masked]
        max_sc[...] = new
        tot_sc[...] = tot_sc[...] * factor + jnp.sum(sum(weights), axis=0, keepdims=True)
        added = lax.dot_general(
            jnp.concatenate(params, axis=1).astype(jnp.bfloat16),
            jnp.concatenate(weights, axis=0).astype(jnp.bfloat16),
            (((1,), (0,)), ((), ())),
            preferred_element_type=jnp.float32,
        )
        sum_sc[...] = sum_sc[...] * factor + added

    def drain_z(o, slot):
        @pl.when(has_up & (o <= z))
        def _():
            to_up(o, slot).wait_send()

        @pl.when(has_dn & (o >= z))
        def _():
            to_dn(o, slot).wait_send()

    def drain(o):
        for slot in range(5):
            drain_z(o, slot)

        @pl.when(is_end(o))
        def _():
            drain_z(o, 5)
            drain_z(o, 6)

        @pl.when(jnp.logical_not(is_end(o)) | (o == z))
        def _():
            to_y(o, 1).wait_send()
            to_y(o, 3).wait_send()

        for slot in (0, 2, 4):
            to_y(o, slot).wait_send()
        for slot in range(3):
            to_core(o, y, slot).wait_send()
            to_core(o, 1 - y, slot).wait_send()

    def sides(dist):
        lo, hi = z - dist, z + dist
        return (
            (lo, (lo >= 0) & (dist >= 0), has_up, to_up),
            (hi, (hi < depth) & (dist > 0), has_dn, to_dn),
        )

    def pass_on(o, slot, further, to):
        to(o, slot).wait_recv()

        @pl.when(further)
        def _():
            to(o, slot).start()

    def same_row(s, q):
        for o, there, further, to in sides(s):

            @pl.when(there)
            def _():
                pass_on(o, q, further, to)
                if q % 2:

                    @pl.when(jnp.logical_not(is_end(o)))
                    def _():
                        to_y(o, q).start()

                    to_core(o, y, q // 2).start()
                else:
                    to_y(o, q).start()
                if q == 1:
                    pass_on(o, 4, further, to)
                    to_y(o, 4).start()
                    to_core(o, y, 2).start()

    def other_row(s, q):
        for o, there, _, to in sides(s - 1):

            @pl.when(there & is_end(o) & (o != z))
            def _():
                if q < 2:
                    from_y(o, 2 * q).wait_recv()
                    if q == 0:
                        from_y(o, 4).wait_recv()
                        to_core(o, 1 - y, 2).start()

                    @pl.when(is_end(z))
                    def _():
                        to(o, 5 + q).wait_recv()

                    to_core(o, 1 - y, q).start()

            @pl.when(there & jnp.logical_not(is_end(o)))
            def _():
                from_y(o, q).wait_recv()
                if q % 2:
                    to_core(o, 1 - y, q // 2).start()
                if q == 1:
                    from_y(o, 4).wait_recv()
                    to_core(o, 1 - y, 2).start()

            @pl.when(there & is_end(o) & (o == z))
            def _():
                from_y(o, (1, 0, 3, 2)[q]).wait_recv()
                if q % 2:
                    to_core(o, 1 - y, q // 2).start()
                else:

                    @pl.when(has_up)
                    def _():
                        to_up(o, 5 + q // 2).start()

                    @pl.when(has_dn)
                    def _():
                        to_dn(o, 5 + q // 2).start()

                if q == 1:
                    from_y(o, 4).wait_recv()
                    to_core(o, 1 - y, 2).start()

    def cross(s, q):
        for o, there, further, to in sides(s):

            @pl.when(there & is_end(o) & (o != z) & further)
            def _():
                to(o, 5 + q).wait_recv()
                to(o, 5 + q).start()

    def settle(dist):
        for o, there, _, _ in sides(dist):

            @pl.when(there)
            def _():
                drain(o)

    def fetch(o, yy, h):
        from_core(o, yy, h).wait_recv()

        @pl.when(h == 0)
        def _():
            from_core(o, yy, 2).wait_recv()

    def turn(i, carry):
        s, q = 1 + i // 4, i % 4
        side, second = q % 2, q // 2
        inner = jnp.where(is_end(z), 0, 1)
        for k in range(4):

            @pl.when(q == k)
            def _():
                if k == 0:
                    settle(s - 3)
                same_row(s, k)
                if k == 0:

                    @pl.when((s == depth) & is_end(z))
                    def _():
                        other_row(s, 0)

                if k < 2:
                    cross(s - 1, k)

        dist = jnp.where(inner == 1, s - 1, s - 1 + second)
        h = jnp.where(inner == 1, second, 1 - second)
        sign = 2 * side - 1
        row_o, other_o = z + sign * dist, z + sign * (dist - 1)
        row_ok = (row_o >= 0) & (row_o < depth) & ((dist > 0) | (q == 0))
        near = (dist > 1) | (side == (depth - 1 - z) // (depth - 1))
        other_ok = (other_o >= 0) & (other_o < depth) & (dist > 0) & near
        closing = (dist == depth) & is_end(z)
        both = row_ok & other_ok
        alone = (row_ok | other_ok) & jnp.logical_not(both | closing) & ((h == 1) | (dist == 0))

        @pl.when(both | alone)
        def _():
            one_at = jnp.where(row_ok, row_o, other_o)
            one_y = jnp.where(row_ok, y, 1 - y)
            two_at = jnp.where(both, other_o, one_at)
            two_y = jnp.where(both, 1 - y, one_y)
            two_h = jnp.where(both, h, 1 - h)
            fetch(one_at, one_y, h)
            fetch(two_at, two_y, two_h)
            absorb(halves(one_at, one_y, h), halves(two_at, two_y, two_h))

        late = s - inner * (1 - second)
        first = jnp.where(inner == 1, 2 * (1 - second), 2 * second)

        @pl.when((side == 1) & (first == 0))
        def _():
            @pl.when((s < depth) | jnp.logical_not(is_end(z)))
            def _():
                other_row(late, 0)

            other_row(late, 1)

        @pl.when((side == 1) & (first == 2))
        def _():
            other_row(late, 2)
            other_row(late, 3)

        return carry

    lax.fori_loop(0, 4 * depth, turn, 0)

    @pl.when(is_end(z))
    def _():
        far = depth - 1 - z

        def close(k, carry):
            @pl.when(k == 1)
            def _():
                for slot in range(3):
                    from_core(far, 1 - y, slot).wait_recv()

            absorb(whole(far, 1 - y, c + k * (1 - 2 * c)))
            return carry

        lax.fori_loop(0, 2, close, 0)

    settle(depth - 2)
    settle(depth - 1)

    out_ref[0:nparam, :] = sum_sc[0:nparam, :]
    out_ref[nparam : nparam + 1, :] = max_sc[...]
    out_ref[nparam + 1 : nparam + 2, :] = tot_sc[...]


def finish(state, mean_ref, lev_ref):
    nparam, rows = mean_ref.shape
    total = state[nparam + 1 : nparam + 2, :]
    mean_ref[...] = state[0:nparam, :] / total
    lev = state[nparam : nparam + 1, :] + jnp.log(total)
    for i in range(rows // LANES):
        lanes = slice(i * LANES, (i + 1) * LANES)
        lev_ref[lanes] = lev[0:1, lanes].reshape(LANES)


def solution(mesh):
    depth = mesh.shape["blk"] // 4

    def on_device(observed, sharpness, obs_class, pattern, evolved, sim_params, sim_class):
        rows, feat = observed.shape
        sims = evolved.shape[0]
        nparam = sim_params.shape[0]
        vmem = pl.BlockSpec(memory_space=pltpu.VMEM)
        hbm = pl.BlockSpec(memory_space=pltpu.HBM)
        dma = pltpu.SemaphoreType.DMA
        arguments = (observed, sharpness, obs_class, pattern, evolved, sim_params, sim_class)
        state = pl.pallas_call(
            functools.partial(gather_and_absorb, depth),
            out_shape=pltpu.VMEM((8, rows), jnp.float32),
            in_specs=[hbm] * 7,
            out_specs=vmem,
            scratch_shapes=[
                pltpu.VMEM((depth, 2, 2, sims, feat), jnp.bfloat16),
                pltpu.VMEM((depth, 2, 2, AUX_ROWS, LANES), jnp.bfloat16),
                pltpu.VMEM((rows, feat), jnp.bfloat16),
                pltpu.VMEM((feat, rows), jnp.bfloat16),
                pltpu.VMEM((rows,), jnp.float32),
                pltpu.VMEM((rows,), jnp.int32),
                pltpu.SMEM(pattern.shape, jnp.int32),
                pltpu.VMEM((nparam, sims), jnp.bfloat16),
                pltpu.VMEM((sims,), jnp.int32),
                pltpu.VMEM((AUX_ROWS, LANES), jnp.float32),
                pltpu.VMEM((1, rows), jnp.float32),
                pltpu.VMEM((1, rows), jnp.int32),
                pltpu.VMEM((1, rows), jnp.float32),
                pltpu.VMEM((1, rows), jnp.float32),
                pltpu.VMEM((1, rows), jnp.float32),
                pltpu.VMEM((AUX_ROWS, rows), jnp.float32),
                dma((7,)),
                dma((7 * depth,)),
                dma((7 * depth,)),
                dma((7 * depth,)),
                dma((5 * depth,)),
                dma((5 * depth,)),
                dma((6 * depth,)),
                dma((6 * depth,)),
                pltpu.SemaphoreType.REGULAR((3,)),
            ],
            compiler_params=pltpu.CompilerParams(
                collective_id=0, has_side_effects=True, vmem_limit_bytes=40 << 20
            ),
        )(*(pltpu.with_memory_space_constraint(a, pltpu.HBM) for a in arguments))
        return pl.pallas_call(
            finish,
            out_shape=(
                jax.ShapeDtypeStruct((nparam, rows), jnp.float32),
                jax.ShapeDtypeStruct((rows,), jnp.float32),
            ),
            in_specs=[vmem],
            out_specs=(vmem, vmem),
            compiler_params=pltpu.CompilerParams(vmem_limit_bytes=4 << 20),
        )(pltpu.with_memory_space_constraint(state, pltpu.VMEM))

    placed = (
        P(("parts", "blk"), None),
        P(("parts", "blk")),
        P(("parts", "blk")),
        P(("parts", "blk"), None),
        P(("parts", "blk"), None),
        P(None, ("parts", "blk")),
        P(("parts", "blk")),
    )
    return jax.shard_map(
        on_device,
        mesh=mesh,
        in_specs=placed,
        out_specs=(P(None, ("parts", "blk")), P(("parts", "blk"))),
        check_vma=False,
    )
```

```python
import functools

import jax
import jax.numpy as jnp
from jax import lax
from jax.experimental import pallas as pl
from jax.experimental.pallas import tpu as pltpu
from jax.sharding import PartitionSpec as P

NEG_START = -1e30
NEG_MASK = -3e38
LANES = 128
AUX_ROWS = 16
MESH = pl.DeviceIdType.MESH


def gather_and_absorb(
    depth,
    obs_hbm,
    sharp_hbm,
    ocls_hbm,
    pat_hbm,
    evo_hbm,
    prm_hbm,
    scls_hbm,
    out_ref,
    gat,
    aux,
    obs,
    obs_t,
    sharp_in,
    ocls_in,
    pat_ref,
    prm_ref,
    scls_in,
    stage,
    sharp_ref,
    ocls_ref,
    base_sc,
    max_sc,
    tot_sc,
    sum_sc,
    local_sem,
    up_send,
    dn_send,
    z_recv,
    y_send,
    y_recv,
    s_send,
    s_recv,
    ready,
):
    me = lax.axis_index("blk")
    z, y, c = me // 4, (me // 2) % 2, me % 2
    rows, feat = obs.shape
    sims = evo_hbm.shape[0]
    half, quarter = sims // 2, sims // 4
    tile_count = pat_hbm.shape[0]
    tile_rows = rows // tile_count
    nparam = prm_hbm.shape[0]

    def blk_of(zz, yy, cc):
        return zz * 4 + yy * 2 + cc

    evo_copy = pltpu.make_async_copy(evo_hbm, gat.at[z, y, c], local_sem.at[0])
    prm_copy = pltpu.make_async_copy(prm_hbm, prm_ref, local_sem.at[1])
    scls_copy = pltpu.make_async_copy(scls_hbm, scls_in, local_sem.at[2])
    obs_copy = pltpu.make_async_copy(obs_hbm, obs, local_sem.at[3])
    sharp_copy = pltpu.make_async_copy(sharp_hbm, sharp_in, local_sem.at[4])
    ocls_copy = pltpu.make_async_copy(ocls_hbm, ocls_in, local_sem.at[5])
    pat_copy = pltpu.make_async_copy(pat_hbm, pat_ref, local_sem.at[6])

    has_up = z < depth - 1
    has_dn = z > 0
    barrier = pltpu.get_barrier_semaphore()

    def greet(dev):
        pl.semaphore_signal(barrier, inc=1, device_id={"blk": dev}, device_id_type=MESH)

    @pl.when(has_up)
    def _():
        greet(blk_of(z + 1, y, c))

    @pl.when(y == 0)
    def _():
        greet(blk_of(z, 1, c))

    @pl.when(c == 0)
    def _():
        greet(blk_of(z, y, 1))

    evo_copy.start()
    prm_copy.start()
    scls_copy.start()

    def is_end(o):
        return (o == 0) | (o == depth - 1)

    def remote(src, dst, dev, send, recv):
        return pltpu.make_async_remote_copy(
            src_ref=src,
            dst_ref=dst,
            send_sem=send,
            recv_sem=recv,
            device_id={"blk": dev},
            device_id_type=MESH,
        )

    def part(o, yy, cc, first, count, own):
        dst = gat.at[o, yy, cc, pl.ds(first, count)]
        return (evo_hbm.at[pl.ds(first, count)] if own else dst), dst

    def along_z(o, slot, own, zz, send):
        if slot == 4:
            src = dst = aux.at[o, y, c]
        elif slot > 4:
            src, dst = part(o, 1 - y, c, (2 * slot - 9) * quarter, quarter, False)
        else:
            src, dst = part(o, y, c, slot * quarter, quarter, own)
        k = o * 7 + slot
        return remote(src, dst, blk_of(zz, y, c), send.at[k], z_recv.at[k])

    def to_up(o, slot, own=False):
        return along_z(o, slot, own, z + 1, up_send)

    def to_dn(o, slot, own=False):
        return along_z(o, slot, own, z - 1, dn_send)

    def across_y(o, yy, slot, own):
        if slot == 4:
            src = dst = aux.at[o, yy, c]
        else:
            src, dst = part(o, yy, c, slot * quarter, quarter, own)
        k = o * 5 + slot
        return remote(src, dst, blk_of(z, 1 - y, c), y_send.at[k], y_recv.at[k])

    def to_y(o, slot, own=False):
        return across_y(o, y, slot, own)

    def from_y(o, slot):
        return across_y(o, 1 - y, slot, False)

    def core_hop(o, yy, cc, slot, own):
        if isinstance(slot, int) and slot == 2:
            src = dst = aux.at[o, yy, cc]
        else:
            src, dst = part(o, yy, cc, slot * half, half, own)
        k = (o * 2 + yy) * 3 + slot
        return remote(src, dst, blk_of(z, y, 1 - c), s_send.at[k], s_recv.at[k])

    def to_core(o, yy, slot, own=False):
        return core_hop(o, yy, c, slot, own)

    def from_core(o, yy, slot):
        return core_hop(o, yy, 1 - c, slot, False)

    def tell(k, dev):
        pl.semaphore_signal(ready.at[k], inc=1, device_id={"blk": dev}, device_id_type=MESH)

    def own_z(to, slots):
        for slot in slots:
            to(z, slot, True).start()

    def own_y(first, last):
        @pl.when(is_end(z))
        def _():
            for slot in (1, 0, 4, 3, 2)[first:last]:
                to_y(z, slot, True).start()

        @pl.when(jnp.logical_not(is_end(z)))
        def _():
            for slot in (0, 1, 4, 2, 3)[first:last]:
                to_y(z, slot, True).start()

    nearer = (z + depth - 1) // depth + y + c

    @pl.when(nearer > 0)
    def _():
        pl.semaphore_wait(barrier, nearer)

    @pl.when(has_dn)
    def _():
        own_z(to_dn, (0, 1))
        tell(0, blk_of(z - 1, y, c))

    @pl.when(y == 1)
    def _():
        own_y(0, 2)
        tell(1, blk_of(z, 0, c))

    @pl.when(c == 1)
    def _():
        tell(2, blk_of(z, y, 0))

    for copy in (obs_copy, sharp_copy, ocls_copy, pat_copy):
        copy.start()

    stage[...] = jnp.zeros_like(stage)
    prm_copy.wait()
    stage[0:nparam, :] = prm_ref[...].astype(jnp.float32)
    scls_copy.wait()
    stage[nparam : nparam + 1, :] = scls_in[...].reshape(1, sims).astype(jnp.float32)
    evo_copy.wait()
    block = gat[z, y, c].astype(jnp.float32)
    own_sq = 0.5 * jnp.sum(block * block, axis=1, keepdims=True)
    left = jnp.broadcast_to(own_sq, (LANES, LANES)).T[0:1, :]
    for k in range(3):
        piece = left.astype(jnp.bfloat16).astype(jnp.float32)
        stage[nparam + 1 + k : nparam + 2 + k, :] = piece
        left = left - piece
    aux[z, y, c] = stage[...].astype(jnp.bfloat16)

    @pl.when(has_dn)
    def _():
        own_z(to_dn, (4, 2, 3))

    @pl.when(y == 1)
    def _():
        own_y(2, 5)

    @pl.when(has_up)
    def _():
        pl.semaphore_wait(ready.at[0], 1)
        own_z(to_up, (0, 1, 4, 2, 3))

    @pl.when(y == 0)
    def _():
        pl.semaphore_wait(ready.at[1], 1)
        own_y(0, 5)

    @pl.when(c == 0)
    def _():
        pl.semaphore_wait(ready.at[2], 1)

    for slot in range(3):
        to_core(z, y, slot, True).start()

    sharp_copy.wait()
    ocls_copy.wait()
    pat_copy.wait()
    obs_copy.wait()
    for i in range(rows // LANES):
        lanes = slice(i * LANES, (i + 1) * LANES)
        sharp_ref[0:1, lanes] = 2.0 * sharp_in[lanes].reshape(1, LANES)
        ocls_ref[0:1, lanes] = ocls_in[lanes].reshape(1, LANES)
        turned = obs[lanes, :].T
        obs_t[:, lanes] = turned
        wide = turned.astype(jnp.float32)
        base_sc[0:1, lanes] = 1.0 * feat - 0.5 * jnp.sum(wide * wide, axis=0, keepdims=True)

    max_sc[...] = jnp.full_like(max_sc, NEG_START)
    tot_sc[...] = jnp.zeros_like(tot_sc)
    sum_sc[...] = jnp.zeros_like(sum_sc)

    first_half = lax.broadcasted_iota(jnp.int32, (AUX_ROWS, LANES), 1) < half

    def pair(*chunks):
        rows_in, packets, sources = [], [], []
        for place, (o, yy, cc, h) in enumerate(chunks):
            rows_in.append(gat[o, yy, cc, pl.ds(pl.multiple_of(h * half, half), half), :])
            packet = aux[o, yy, cc].astype(jnp.float32)
            packets.append(jnp.where(h == place, packet, pltpu.roll(packet, half, 1)))
            sources.append((blk_of(o, yy, cc), half))
        return rows_in, jnp.where(first_half, packets[0], packets[1]), sources

    def whole(o, yy, cc):
        return [gat[o, yy, cc]], aux[o, yy, cc].astype(jnp.float32), [(blk_of(o, yy, cc), sims)]

    def absorb(*parts):
        lhs, half_sq, classes, params = [], [], [], []
        for rows_in, packet, _ in parts:
            lhs.extend(rows_in)
            params.append(packet)
            column = packet[0:8, :].T
            classes.append(column[:, nparam : nparam + 1])
            half_sq.append(
                column[:, nparam + 1 : nparam + 2]
                + column[:, nparam + 2 : nparam + 3]
                + column[:, nparam + 3 : nparam + 4]
            )
        product = lax.dot_general(
            jnp.concatenate(lhs, axis=0),
            obs_t[...],
            (((1,), (0,)), ((), ())),
            preferred_element_type=jnp.float32,
        )
        sharp2 = sharp_ref[...]
        base = base_sc[...]
        masked = []
        for p, (_, _, sources) in enumerate(parts):
            row = 0
            for source, count in sources:
                wanted = jnp.concatenate(
                    [
                        jnp.where(
                            pat_ref[i, source] == 1,
                            ocls_ref[0:1, i * tile_rows : (i + 1) * tile_rows],
                            -1,
                        )
                        for i in range(tile_count)
                    ],
                    axis=1,
                ).astype(jnp.float32)
                mine = slice(row, row + count)
                span = slice(p * sims + row, p * sims + row + count)
                score = ((product[span] - half_sq[p][mine]) + base) * sharp2
                masked.append(jnp.where(classes[p][mine] == wanted, score, NEG_MASK))
                row += count
        top = functools.reduce(jnp.maximum, masked)
        old = max_sc[...]
        new = jnp.maximum(old, jnp.max(top, axis=0, keepdims=True))
        factor = jnp.exp(old - new)
        weights = [jnp.exp(m - new) for m in masked]
        max_sc[...] = new
        tot_sc[...] = tot_sc[...] * factor + jnp.sum(sum(weights), axis=0, keepdims=True)
        added = lax.dot_general(
            jnp.concatenate(params, axis=1).astype(jnp.bfloat16),
            jnp.concatenate(weights, axis=0).astype(jnp.bfloat16),
            (((1,), (0,)), ((), ())),
            preferred_element_type=jnp.float32,
        )
        sum_sc[...] = sum_sc[...] * factor + added

    def drain_z(o, slot):
        @pl.when(has_up & (o <= z))
        def _():
            to_up(o, slot).wait_send()

        @pl.when(has_dn & (o >= z))
        def _():
            to_dn(o, slot).wait_send()

    def drain(o):
        for slot in range(5):
            drain_z(o, slot)

        @pl.when(is_end(o))
        def _():
            drain_z(o, 5)
            drain_z(o, 6)

        @pl.when(jnp.logical_not(is_end(o)) | (o == z))
        def _():
            to_y(o, 1).wait_send()
            to_y(o, 3).wait_send()

        for slot in (0, 2, 4):
            to_y(o, slot).wait_send()
        for slot in range(3):
            to_core(o, y, slot).wait_send()
            to_core(o, 1 - y, slot).wait_send()

    def sides(dist):
        lo, hi = z - dist, z + dist
        return (
            (lo, (lo >= 0) & (dist >= 0), has_up, to_up),
            (hi, (hi < depth) & (dist > 0), has_dn, to_dn),
        )

    def pass_on(o, slot, further, to):
        to(o, slot).wait_recv()

        @pl.when(further)
        def _():
            to(o, slot).start()

    def same_row(s, q):
        for o, there, further, to in sides(s):

            @pl.when(there)
            def _():
                pass_on(o, q, further, to)
                if q % 2:

                    @pl.when(jnp.logical_not(is_end(o)))
                    def _():
                        to_y(o, q).start()

                    to_core(o, y, q // 2).start()
                else:
                    to_y(o, q).start()
                if q == 1:
                    pass_on(o, 4, further, to)
                    to_y(o, 4).start()
                    to_core(o, y, 2).start()

    def other_row(s, q):
        for o, there, _, to in sides(s - 1):

            @pl.when(there & is_end(o) & (o != z))
            def _():
                if q < 2:
                    from_y(o, 2 * q).wait_recv()
                    if q == 0:
                        from_y(o, 4).wait_recv()
                        to_core(o, 1 - y, 2).start()

                    @pl.when(is_end(z))
                    def _():
                        to(o, 5 + q).wait_recv()

                    to_core(o, 1 - y, q).start()

            @pl.when(there & jnp.logical_not(is_end(o)))
            def _():
                from_y(o, q).wait_recv()
                if q % 2:
                    to_core(o, 1 - y, q // 2).start()
                if q == 1:
                    from_y(o, 4).wait_recv()
                    to_core(o, 1 - y, 2).start()

            @pl.when(there & is_end(o) & (o == z))
            def _():
                from_y(o, (1, 0, 3, 2)[q]).wait_recv()
                if q % 2:
                    to_core(o, 1 - y, q // 2).start()
                else:

                    @pl.when(has_up)
                    def _():
                        to_up(o, 5 + q // 2).start()

                    @pl.when(has_dn)
                    def _():
                        to_dn(o, 5 + q // 2).start()

                if q == 1:
                    from_y(o, 4).wait_recv()
                    to_core(o, 1 - y, 2).start()

    def cross(s, q):
        for o, there, further, to in sides(s):

            @pl.when(there & is_end(o) & (o != z) & further)
            def _():
                to(o, 5 + q).wait_recv()
                to(o, 5 + q).start()

    def settle(dist):
        for o, there, _, _ in sides(dist):

            @pl.when(there)
            def _():
                drain(o)

    def fetch(o, yy, h):
        from_core(o, yy, h).wait_recv()

        @pl.when(h == 0)
        def _():
            from_core(o, yy, 2).wait_recv()

    far = depth - 1 - z
    before = z + (depth - 2) * (1 - 2 * (z // (depth - 1)))

    def turn(i, carry):
        s, q = 1 + i // 4, i % 4
        side, second = q % 2, q // 2
        inner = jnp.where(is_end(z), 0, 1)
        for k in range(4):

            @pl.when(q == k)
            def _():
                if k == 0:
                    settle(s - 3)
                same_row(s, k)
                if k < 2:
                    cross(s - 1, k)

        dist = jnp.where(inner == 1, s - 1, s - 1 + second)
        h = jnp.where(inner == 1, second, 1 - second)
        sign = 2 * side - 1
        row_o, other_o = z + sign * dist, z + sign * (dist - 1)
        row_ok = (row_o >= 0) & (row_o < depth) & ((dist > 0) | (q == 0))
        near = (dist > 1) | (side == (depth - 1 - z) // (depth - 1))
        other_ok = (other_o >= 0) & (other_o < depth) & (dist > 0) & near
        closing = (dist == depth) & is_end(z)
        ending = (s == depth) & is_end(z)
        last = ending & (q == 1)
        both = row_ok & other_ok & jnp.logical_not(ending)
        alone = (row_ok | other_ok) & jnp.logical_not(both | closing | ending)

        @pl.when(last)
        def _():
            absorb(pair((far, y, c, 1), (before, 1 - y, c, 1)))
            other_row(s, 0)
            from_core(far, y, 1).wait_recv()
            from_core(before, 1 - y, 1).wait_recv()
            absorb(pair((far, y, 1 - c, 1), (before, 1 - y, 1 - c, 1)))
            other_row(s, 1)
            absorb(whole(far, 1 - y, c))

        one_at = jnp.where(row_ok, row_o, other_o)
        one_y = jnp.where(row_ok, y, 1 - y)
        two_at = jnp.where(both, other_o, one_at)
        two_y = jnp.where(both, 1 - y, one_y)
        two_h = jnp.where(both, h, 1 - h)
        usual = (both | (alone & ((h == 1) | (dist == 0)))) & jnp.logical_not(last)

        @pl.when(usual)
        def _():
            fetch(one_at, one_y, h)
            fetch(two_at, two_y, two_h)

        @pl.when(usual)
        def _():
            absorb(
                pair((one_at, one_y, 0, h), (one_at, one_y, 1, h)),
                pair((two_at, two_y, 0, two_h), (two_at, two_y, 1, two_h)),
            )

        late = s - inner * (1 - second)
        first = jnp.where(inner == 1, 2 * (1 - second), 2 * second)

        @pl.when((side == 1) & (first == 0) & jnp.logical_not(ending))
        def _():
            other_row(late, 0)
            other_row(late, 1)

        @pl.when((side == 1) & (first == 2) & jnp.logical_not(ending))
        def _():
            other_row(late, 2)
            other_row(late, 3)

        return carry

    lax.fori_loop(0, 4 * depth, turn, 0)

    @pl.when(is_end(z))
    def _():
        settle(depth - 2)
        settle(depth - 1)
        for slot in range(3):
            from_core(far, 1 - y, slot).wait_recv()
        absorb(whole(far, 1 - y, 1 - c))

    @pl.when(jnp.logical_not(is_end(z)))
    def _():
        settle(depth - 2)

    out_ref[0:nparam, :] = sum_sc[0:nparam, :]
    out_ref[nparam : nparam + 1, :] = max_sc[...]
    out_ref[nparam + 1 : nparam + 2, :] = tot_sc[...]


def finish(state, mean_ref, lev_ref):
    nparam, rows = mean_ref.shape
    total = state[nparam + 1 : nparam + 2, :]
    mean_ref[...] = state[0:nparam, :] / total
    lev = state[nparam : nparam + 1, :] + jnp.log(total)
    for i in range(rows // LANES):
        lanes = slice(i * LANES, (i + 1) * LANES)
        lev_ref[lanes] = lev[0:1, lanes].reshape(LANES)


def solution(mesh):
    depth = mesh.shape["blk"] // 4

    def on_device(observed, sharpness, obs_class, pattern, evolved, sim_params, sim_class):
        rows, feat = observed.shape
        sims = evolved.shape[0]
        nparam = sim_params.shape[0]
        vmem = pl.BlockSpec(memory_space=pltpu.VMEM)
        hbm = pl.BlockSpec(memory_space=pltpu.HBM)
        dma = pltpu.SemaphoreType.DMA
        arguments = (observed, sharpness, obs_class, pattern, evolved, sim_params, sim_class)
        state = pl.pallas_call(
            functools.partial(gather_and_absorb, depth),
            out_shape=pltpu.VMEM((8, rows), jnp.float32),
            in_specs=[hbm] * 7,
            out_specs=vmem,
            scratch_shapes=[
                pltpu.VMEM((depth, 2, 2, sims, feat), jnp.bfloat16),
                pltpu.VMEM((depth, 2, 2, AUX_ROWS, LANES), jnp.bfloat16),
                pltpu.VMEM((rows, feat), jnp.bfloat16),
                pltpu.VMEM((feat, rows), jnp.bfloat16),
                pltpu.VMEM((rows,), jnp.float32),
                pltpu.VMEM((rows,), jnp.int32),
                pltpu.SMEM(pattern.shape, jnp.int32),
                pltpu.VMEM((nparam, sims), jnp.bfloat16),
                pltpu.VMEM((sims,), jnp.int32),
                pltpu.VMEM((AUX_ROWS, LANES), jnp.float32),
                pltpu.VMEM((1, rows), jnp.float32),
                pltpu.VMEM((1, rows), jnp.int32),
                pltpu.VMEM((1, rows), jnp.float32),
                pltpu.VMEM((1, rows), jnp.float32),
                pltpu.VMEM((1, rows), jnp.float32),
                pltpu.VMEM((AUX_ROWS, rows), jnp.float32),
                dma((7,)),
                dma((7 * depth,)),
                dma((7 * depth,)),
                dma((7 * depth,)),
                dma((5 * depth,)),
                dma((5 * depth,)),
                dma((6 * depth,)),
                dma((6 * depth,)),
                pltpu.SemaphoreType.REGULAR((3,)),
            ],
            compiler_params=pltpu.CompilerParams(
                collective_id=0, has_side_effects=True, vmem_limit_bytes=40 << 20
            ),
        )(*(pltpu.with_memory_space_constraint(a, pltpu.HBM) for a in arguments))
        return pl.pallas_call(
            finish,
            out_shape=(
                jax.ShapeDtypeStruct((nparam, rows), jnp.float32),
                jax.ShapeDtypeStruct((rows,), jnp.float32),
            ),
            in_specs=[vmem],
            out_specs=(vmem, vmem),
            compiler_params=pltpu.CompilerParams(vmem_limit_bytes=4 << 20),
        )(pltpu.with_memory_space_constraint(state, pltpu.VMEM))

    placed = (
        P(("parts", "blk"), None),
        P(("parts", "blk")),
        P(("parts", "blk")),
        P(("parts", "blk"), None),
        P(("parts", "blk"), None),
        P(None, ("parts", "blk")),
        P(("parts", "blk")),
    )
    return jax.shard_map(
        on_device,
        mesh=mesh,
        in_specs=placed,
        out_specs=(P(None, ("parts", "blk")), P(("parts", "blk"))),
        check_vma=False,
    )
```

```python
import functools

import jax
import jax.numpy as jnp
from jax import lax
from jax.experimental import pallas as pl
from jax.experimental.pallas import tpu as pltpu
from jax.sharding import PartitionSpec as P

NEG_START = -1e30
NEG_MASK = -3e38
LANES = 128
AUX_ROWS = 16
MESH = pl.DeviceIdType.MESH


def gather_and_absorb(
    depth,
    obs_hbm,
    sharp_hbm,
    ocls_hbm,
    pat_hbm,
    evo_hbm,
    prm_hbm,
    scls_hbm,
    out_ref,
    gat,
    aux,
    obs,
    obs_t,
    sharp_in,
    ocls_in,
    pat_ref,
    prm_ref,
    scls_in,
    stage,
    sharp_ref,
    ocls_ref,
    base_sc,
    max_sc,
    tot_sc,
    sum_sc,
    local_sem,
    up_send,
    dn_send,
    z_recv,
    y_send,
    y_recv,
    s_send,
    s_recv,
    ready,
):
    me = lax.axis_index("blk")
    z, y, c = me // 4, (me // 2) % 2, me % 2
    rows, feat = obs.shape
    sims = evo_hbm.shape[0]
    half, quarter = sims // 2, sims // 4
    tile_count = pat_hbm.shape[0]
    tile_rows = rows // tile_count
    nparam = prm_hbm.shape[0]

    def blk_of(zz, yy, cc):
        return zz * 4 + yy * 2 + cc

    evo_copy = pltpu.make_async_copy(evo_hbm, gat.at[z, y, c], local_sem.at[0])
    prm_copy = pltpu.make_async_copy(prm_hbm, prm_ref, local_sem.at[1])
    scls_copy = pltpu.make_async_copy(scls_hbm, scls_in, local_sem.at[2])
    obs_copy = pltpu.make_async_copy(obs_hbm, obs, local_sem.at[3])
    sharp_copy = pltpu.make_async_copy(sharp_hbm, sharp_in, local_sem.at[4])
    ocls_copy = pltpu.make_async_copy(ocls_hbm, ocls_in, local_sem.at[5])
    pat_copy = pltpu.make_async_copy(pat_hbm, pat_ref, local_sem.at[6])

    has_up = z < depth - 1
    has_dn = z > 0
    barrier = pltpu.get_barrier_semaphore()

    def greet(dev):
        pl.semaphore_signal(barrier, inc=1, device_id={"blk": dev}, device_id_type=MESH)

    @pl.when(has_up)
    def _():
        greet(blk_of(z + 1, y, c))

    @pl.when(y == 0)
    def _():
        greet(blk_of(z, 1, c))

    @pl.when(c == 0)
    def _():
        greet(blk_of(z, y, 1))

    evo_copy.start()
    prm_copy.start()
    scls_copy.start()

    def is_end(o):
        return (o == 0) | (o == depth - 1)

    def remote(src, dst, dev, send, recv):
        return pltpu.make_async_remote_copy(
            src_ref=src,
            dst_ref=dst,
            send_sem=send,
            recv_sem=recv,
            device_id={"blk": dev},
            device_id_type=MESH,
        )

    def part(o, yy, cc, first, count, own):
        dst = gat.at[o, yy, cc, pl.ds(first, count)]
        return (evo_hbm.at[pl.ds(first, count)] if own else dst), dst

    def along_z(o, slot, own, zz, send):
        if slot == 4:
            src = dst = aux.at[o, y, c]
        elif slot > 4:
            src, dst = part(o, 1 - y, c, (2 * slot - 9) * quarter, quarter, False)
        else:
            src, dst = part(o, y, c, slot * quarter, quarter, own)
        k = o * 7 + slot
        return remote(src, dst, blk_of(zz, y, c), send.at[k], z_recv.at[k])

    def to_up(o, slot, own=False):
        return along_z(o, slot, own, z + 1, up_send)

    def to_dn(o, slot, own=False):
        return along_z(o, slot, own, z - 1, dn_send)

    def across_y(o, yy, slot, own):
        if slot == 4:
            src = dst = aux.at[o, yy, c]
        else:
            src, dst = part(o, yy, c, slot * quarter, quarter, own)
        k = o * 5 + slot
        return remote(src, dst, blk_of(z, 1 - y, c), y_send.at[k], y_recv.at[k])

    def to_y(o, slot, own=False):
        return across_y(o, y, slot, own)

    def from_y(o, slot):
        return across_y(o, 1 - y, slot, False)

    def core_hop(o, yy, cc, slot, own):
        if isinstance(slot, int) and slot == 2:
            src = dst = aux.at[o, yy, cc]
        else:
            src, dst = part(o, yy, cc, slot * half, half, own)
        k = (o * 2 + yy) * 3 + slot
        return remote(src, dst, blk_of(z, y, 1 - c), s_send.at[k], s_recv.at[k])

    def to_core(o, yy, slot, own=False):
        return core_hop(o, yy, c, slot, own)

    def from_core(o, yy, slot):
        return core_hop(o, yy, 1 - c, slot, False)

    def tell(k, dev):
        pl.semaphore_signal(ready.at[k], inc=1, device_id={"blk": dev}, device_id_type=MESH)

    def own_z(to, slots):
        for slot in slots:
            to(z, slot, True).start()

    def own_y(first, last):
        @pl.when(is_end(z))
        def _():
            for slot in (1, 0, 4, 3, 2)[first:last]:
                to_y(z, slot, True).start()

        @pl.when(jnp.logical_not(is_end(z)))
        def _():
            for slot in (0, 1, 4, 2, 3)[first:last]:
                to_y(z, slot, True).start()

    nearer = (z + depth - 1) // depth + y + c

    @pl.when(nearer > 0)
    def _():
        pl.semaphore_wait(barrier, nearer)

    @pl.when(has_dn)
    def _():
        own_z(to_dn, (0, 1))
        tell(0, blk_of(z - 1, y, c))

    @pl.when(y == 1)
    def _():
        own_y(0, 2)
        tell(1, blk_of(z, 0, c))

    @pl.when(c == 1)
    def _():
        tell(2, blk_of(z, y, 0))

    for copy in (obs_copy, sharp_copy, ocls_copy, pat_copy):
        copy.start()

    stage[...] = jnp.zeros_like(stage)
    prm_copy.wait()
    stage[0:nparam, :] = prm_ref[...].astype(jnp.float32)
    scls_copy.wait()
    stage[nparam : nparam + 1, :] = scls_in[...].reshape(1, sims).astype(jnp.float32)
    evo_copy.wait()
    block = gat[z, y, c].astype(jnp.float32)
    own_sq = 0.5 * jnp.sum(block * block, axis=1, keepdims=True)
    left = jnp.broadcast_to(own_sq, (LANES, LANES)).T[0:1, :]
    for k in range(3):
        piece = left.astype(jnp.bfloat16).astype(jnp.float32)
        stage[nparam + 1 + k : nparam + 2 + k, :] = piece
        left = left - piece
    aux[z, y, c] = stage[...].astype(jnp.bfloat16)

    @pl.when(has_dn)
    def _():
        own_z(to_dn, (4, 2, 3))

    @pl.when(y == 1)
    def _():
        own_y(2, 5)

    @pl.when(has_up)
    def _():
        pl.semaphore_wait(ready.at[0], 1)
        own_z(to_up, (0, 1, 4, 2, 3))

    @pl.when(y == 0)
    def _():
        pl.semaphore_wait(ready.at[1], 1)
        own_y(0, 5)

    @pl.when(c == 0)
    def _():
        pl.semaphore_wait(ready.at[2], 1)

    for slot in range(3):
        to_core(z, y, slot, True).start()

    sharp_copy.wait()
    ocls_copy.wait()
    pat_copy.wait()
    obs_copy.wait()
    for i in range(rows // LANES):
        lanes = slice(i * LANES, (i + 1) * LANES)
        sharp_ref[0:1, lanes] = 2.0 * sharp_in[lanes].reshape(1, LANES)
        ocls_ref[0:1, lanes] = ocls_in[lanes].reshape(1, LANES)
        turned = obs[lanes, :].T
        obs_t[:, lanes] = turned
        wide = turned.astype(jnp.float32)
        base_sc[0:1, lanes] = 1.0 * feat - 0.5 * jnp.sum(wide * wide, axis=0, keepdims=True)

    max_sc[...] = jnp.full_like(max_sc, NEG_START)
    tot_sc[...] = jnp.zeros_like(tot_sc)
    sum_sc[...] = jnp.zeros_like(sum_sc)

    first_half = lax.broadcasted_iota(jnp.int32, (AUX_ROWS, LANES), 1) < half

    def pair(*chunks):
        rows_in, packets, sources = [], [], []
        for place, (o, yy, cc, h) in enumerate(chunks):
            rows_in.append(gat[o, yy, cc, pl.ds(pl.multiple_of(h * half, half), half), :])
            packet = aux[o, yy, cc].astype(jnp.float32)
            packets.append(jnp.where(h == place, packet, pltpu.roll(packet, half, 1)))
            sources.append((blk_of(o, yy, cc), half))
        return rows_in, jnp.where(first_half, packets[0], packets[1]), sources

    def whole(o, yy, cc):
        return [gat[o, yy, cc]], aux[o, yy, cc].astype(jnp.float32), [(blk_of(o, yy, cc), sims)]

    def absorb(*parts):
        lhs, half_sq, classes, params = [], [], [], []
        for rows_in, packet, _ in parts:
            lhs.extend(rows_in)
            params.append(packet)
            column = packet[0:8, :].T
            classes.append(column[:, nparam : nparam + 1])
            half_sq.append(
                column[:, nparam + 1 : nparam + 2]
                + column[:, nparam + 2 : nparam + 3]
                + column[:, nparam + 3 : nparam + 4]
            )
        product = lax.dot_general(
            jnp.concatenate(lhs, axis=0),
            obs_t[...],
            (((1,), (0,)), ((), ())),
            preferred_element_type=jnp.float32,
        )
        sharp2 = sharp_ref[...]
        base = base_sc[...]
        masked = []
        for p, (_, _, sources) in enumerate(parts):
            row = 0
            for source, count in sources:
                wanted = jnp.concatenate(
                    [
                        jnp.where(
                            pat_ref[i, source] == 1,
                            ocls_ref[0:1, i * tile_rows : (i + 1) * tile_rows],
                            -1,
                        )
                        for i in range(tile_count)
                    ],
                    axis=1,
                ).astype(jnp.float32)
                mine = slice(row, row + count)
                span = slice(p * sims + row, p * sims + row + count)
                score = ((product[span] - half_sq[p][mine]) + base) * sharp2
                masked.append(jnp.where(classes[p][mine] == wanted, score, NEG_MASK))
                row += count
        top = functools.reduce(jnp.maximum, masked)
        old = max_sc[...]
        new = jnp.maximum(old, jnp.max(top, axis=0, keepdims=True))
        factor = jnp.exp(old - new)
        weights = [jnp.exp(m - new) for m in masked]
        max_sc[...] = new
        tot_sc[...] = tot_sc[...] * factor + jnp.sum(sum(weights), axis=0, keepdims=True)
        added = lax.dot_general(
            jnp.concatenate(params, axis=1).astype(jnp.bfloat16),
            jnp.concatenate(weights, axis=0).astype(jnp.bfloat16),
            (((1,), (0,)), ((), ())),
            preferred_element_type=jnp.float32,
        )
        sum_sc[...] = sum_sc[...] * factor + added

    def drain_z(o, slot):
        @pl.when(has_up & (o <= z))
        def _():
            to_up(o, slot).wait_send()

        @pl.when(has_dn & (o >= z))
        def _():
            to_dn(o, slot).wait_send()

    def drain(o):
        for slot in range(5):
            drain_z(o, slot)

        @pl.when(is_end(o))
        def _():
            drain_z(o, 5)
            drain_z(o, 6)

        @pl.when(jnp.logical_not(is_end(o)) | (o == z))
        def _():
            to_y(o, 1).wait_send()
            to_y(o, 3).wait_send()

        for slot in (0, 2, 4):
            to_y(o, slot).wait_send()
        for slot in range(3):
            to_core(o, y, slot).wait_send()
            to_core(o, 1 - y, slot).wait_send()

    def sides(dist):
        lo, hi = z - dist, z + dist
        return (
            (lo, (lo >= 0) & (dist >= 0), has_up, to_up),
            (hi, (hi < depth) & (dist > 0), has_dn, to_dn),
        )

    def pass_on(o, slot, further, to):
        to(o, slot).wait_recv()

        @pl.when(further)
        def _():
            to(o, slot).start()

    def same_row(s, q):
        for o, there, further, to in sides(s):

            @pl.when(there)
            def _():
                pass_on(o, q, further, to)
                if q % 2:

                    @pl.when(jnp.logical_not(is_end(o)))
                    def _():
                        to_y(o, q).start()

                    to_core(o, y, q // 2).start()
                else:
                    to_y(o, q).start()
                if q == 1:
                    pass_on(o, 4, further, to)
                    to_y(o, 4).start()
                    to_core(o, y, 2).start()

    def other_row(s, q):
        for o, there, _, to in sides(s - 1):

            @pl.when(there & is_end(o) & (o != z))
            def _():
                if q < 2:
                    from_y(o, 2 * q).wait_recv()
                    if q == 0:
                        from_y(o, 4).wait_recv()
                        to_core(o, 1 - y, 2).start()

                    @pl.when(is_end(z))
                    def _():
                        to(o, 5 + q).wait_recv()

                    to_core(o, 1 - y, q).start()

            @pl.when(there & jnp.logical_not(is_end(o)))
            def _():
                from_y(o, q).wait_recv()
                if q % 2:
                    to_core(o, 1 - y, q // 2).start()
                if q == 1:
                    from_y(o, 4).wait_recv()
                    to_core(o, 1 - y, 2).start()

            @pl.when(there & is_end(o) & (o == z))
            def _():
                from_y(o, (1, 0, 3, 2)[q]).wait_recv()
                if q % 2:
                    to_core(o, 1 - y, q // 2).start()
                else:

                    @pl.when(has_up)
                    def _():
                        to_up(o, 5 + q // 2).start()

                    @pl.when(has_dn)
                    def _():
                        to_dn(o, 5 + q // 2).start()

                if q == 1:
                    from_y(o, 4).wait_recv()
                    to_core(o, 1 - y, 2).start()

    def cross(s, q):
        for o, there, further, to in sides(s):

            @pl.when(there & is_end(o) & (o != z) & further)
            def _():
                to(o, 5 + q).wait_recv()
                to(o, 5 + q).start()

    def settle(dist):
        for o, there, _, _ in sides(dist):

            @pl.when(there)
            def _():
                drain(o)

    def fetch(o, yy, h):
        from_core(o, yy, h).wait_recv()

        @pl.when(h == 0)
        def _():
            from_core(o, yy, 2).wait_recv()

    far = depth - 1 - z
    before = z + (depth - 2) * (1 - 2 * (z // (depth - 1)))

    def turn(i, carry):
        s, q = 1 + i // 4, i % 4
        side, second = q % 2, q // 2
        inner = jnp.where(is_end(z), 0, 1)
        for k in range(4):

            @pl.when(q == k)
            def _():
                if k == 0:
                    settle(s - 3)
                same_row(s, k)
                if k < 2:
                    cross(s - 1, k)

        dist = jnp.where(inner == 1, s - 1, s - 1 + second)
        h = jnp.where(inner == 1, second, 1 - second)
        sign = 2 * side - 1
        row_o, other_o = z + sign * dist, z + sign * (dist - 1)
        row_ok = (row_o >= 0) & (row_o < depth) & ((dist > 0) | (q == 0))
        near = (dist > 1) | (side == (depth - 1 - z) // (depth - 1))
        other_ok = (other_o >= 0) & (other_o < depth) & (dist > 0) & near
        closing = (dist == depth) & is_end(z)
        ending = (s == depth) & is_end(z)
        last = ending & (q == 1)
        both = row_ok & other_ok & jnp.logical_not(ending)
        alone = (row_ok | other_ok) & jnp.logical_not(both | closing | ending)

        for k in range(2):

            @pl.when((q == 2 * k + 1) & (inner == 0) & (s < depth))
            def _():
                other_row(s, 2 * k)
                other_row(s, 2 * k + 1)

        @pl.when(last)
        def _():
            absorb(pair((far, y, c, 1), (before, 1 - y, c, 1)))
            other_row(s, 0)
            from_core(far, y, 1).wait_recv()
            from_core(before, 1 - y, 1).wait_recv()
            absorb(pair((far, y, 1 - c, 1), (before, 1 - y, 1 - c, 1)))
            other_row(s, 1)
            absorb(whole(far, 1 - y, c))

        one_at = jnp.where(row_ok, row_o, other_o)
        one_y = jnp.where(row_ok, y, 1 - y)
        two_at = jnp.where(both, other_o, one_at)
        two_y = jnp.where(both, 1 - y, one_y)
        two_h = jnp.where(both, h, 1 - h)
        usual = (both | (alone & ((h == 1) | (dist == 0)))) & jnp.logical_not(last)

        @pl.when(usual)
        def _():
            fetch(one_at, one_y, h)
            fetch(two_at, two_y, two_h)

        @pl.when(usual)
        def _():
            absorb(
                pair((one_at, one_y, 0, h), (one_at, one_y, 1, h)),
                pair((two_at, two_y, 0, two_h), (two_at, two_y, 1, two_h)),
            )

        @pl.when((q == 1) & (inner == 1))
        def _():
            other_row(s - 1, 2)
            other_row(s - 1, 3)

        @pl.when((q == 3) & (inner == 1))
        def _():
            other_row(s, 0)
            other_row(s, 1)

        return carry

    lax.fori_loop(0, 4 * depth, turn, 0)

    @pl.when(is_end(z))
    def _():
        settle(depth - 2)
        for slot in range(3):
            from_core(far, 1 - y, slot).wait_recv()
        absorb(whole(far, 1 - y, 1 - c))
        settle(depth - 1)

    @pl.when(jnp.logical_not(is_end(z)))
    def _():
        settle(depth - 2)

    out_ref[0:nparam, :] = sum_sc[0:nparam, :]
    out_ref[nparam : nparam + 1, :] = max_sc[...]
    out_ref[nparam + 1 : nparam + 2, :] = tot_sc[...]


def finish(state, mean_ref, lev_ref):
    nparam, rows = mean_ref.shape
    total = state[nparam + 1 : nparam + 2, :]
    mean_ref[...] = state[0:nparam, :] / total
    lev = state[nparam : nparam + 1, :] + jnp.log(total)
    for i in range(rows // LANES):
        lanes = slice(i * LANES, (i + 1) * LANES)
        lev_ref[lanes] = lev[0:1, lanes].reshape(LANES)


def solution(mesh):
    depth = mesh.shape["blk"] // 4

    def on_device(observed, sharpness, obs_class, pattern, evolved, sim_params, sim_class):
        rows, feat = observed.shape
        sims = evolved.shape[0]
        nparam = sim_params.shape[0]
        vmem = pl.BlockSpec(memory_space=pltpu.VMEM)
        hbm = pl.BlockSpec(memory_space=pltpu.HBM)
        dma = pltpu.SemaphoreType.DMA
        arguments = (observed, sharpness, obs_class, pattern, evolved, sim_params, sim_class)
        state = pl.pallas_call(
            functools.partial(gather_and_absorb, depth),
            out_shape=pltpu.VMEM((8, rows), jnp.float32),
            in_specs=[hbm] * 7,
            out_specs=vmem,
            scratch_shapes=[
                pltpu.VMEM((depth, 2, 2, sims, feat), jnp.bfloat16),
                pltpu.VMEM((depth, 2, 2, AUX_ROWS, LANES), jnp.bfloat16),
                pltpu.VMEM((rows, feat), jnp.bfloat16),
                pltpu.VMEM((feat, rows), jnp.bfloat16),
                pltpu.VMEM((rows,), jnp.float32),
                pltpu.VMEM((rows,), jnp.int32),
                pltpu.SMEM(pattern.shape, jnp.int32),
                pltpu.VMEM((nparam, sims), jnp.bfloat16),
                pltpu.VMEM((sims,), jnp.int32),
                pltpu.VMEM((AUX_ROWS, LANES), jnp.float32),
                pltpu.VMEM((1, rows), jnp.float32),
                pltpu.VMEM((1, rows), jnp.int32),
                pltpu.VMEM((1, rows), jnp.float32),
                pltpu.VMEM((1, rows), jnp.float32),
                pltpu.VMEM((1, rows), jnp.float32),
                pltpu.VMEM((AUX_ROWS, rows), jnp.float32),
                dma((7,)),
                dma((7 * depth,)),
                dma((7 * depth,)),
                dma((7 * depth,)),
                dma((5 * depth,)),
                dma((5 * depth,)),
                dma((6 * depth,)),
                dma((6 * depth,)),
                pltpu.SemaphoreType.REGULAR((3,)),
            ],
            compiler_params=pltpu.CompilerParams(
                collective_id=0, has_side_effects=True, vmem_limit_bytes=40 << 20
            ),
        )(*(pltpu.with_memory_space_constraint(a, pltpu.HBM) for a in arguments))
        return pl.pallas_call(
            finish,
            out_shape=(
                jax.ShapeDtypeStruct((nparam, rows), jnp.float32),
                jax.ShapeDtypeStruct((rows,), jnp.float32),
            ),
            in_specs=[vmem],
            out_specs=(vmem, vmem),
            compiler_params=pltpu.CompilerParams(vmem_limit_bytes=4 << 20),
        )(pltpu.with_memory_space_constraint(state, pltpu.VMEM))

    placed = (
        P(("parts", "blk"), None),
        P(("parts", "blk")),
        P(("parts", "blk")),
        P(("parts", "blk"), None),
        P(("parts", "blk"), None),
        P(None, ("parts", "blk")),
        P(("parts", "blk")),
    )
    return jax.shard_map(
        on_device,
        mesh=mesh,
        in_specs=placed,
        out_specs=(P(None, ("parts", "blk")), P(("parts", "blk"))),
        check_vma=False,
    )
```

```python
import functools

import jax
import jax.numpy as jnp
from jax import lax
from jax.experimental import pallas as pl
from jax.experimental.pallas import tpu as pltpu
from jax.sharding import PartitionSpec as P

NEG_START = -1e30
NEG_MASK = -3e38
LANES = 128
AUX_ROWS = 16
LOG2_E = 1.4426950408889634
LN_2 = 0.6931471805599453
MESH = pl.DeviceIdType.MESH


def gather_and_absorb(
    depth,
    obs_hbm,
    sharp_hbm,
    ocls_hbm,
    pat_hbm,
    evo_hbm,
    prm_hbm,
    scls_hbm,
    out_ref,
    gat,
    aux,
    obs,
    obs_t,
    sharp_in,
    ocls_in,
    pat_ref,
    prm_ref,
    scls_in,
    stage,
    sharp_ref,
    ocls_ref,
    base_sc,
    max_sc,
    tot_sc,
    sum_sc,
    local_sem,
    up_send,
    dn_send,
    z_recv,
    y_send,
    y_recv,
    s_send,
    s_recv,
    ready,
):
    me = lax.axis_index("blk")
    z, y, c = me // 4, (me // 2) % 2, me % 2
    rows, feat = obs.shape
    sims = evo_hbm.shape[0]
    half, quarter = sims // 2, sims // 4
    tile_count = pat_hbm.shape[0]
    tile_rows = rows // tile_count
    nparam = prm_hbm.shape[0]

    def blk_of(zz, yy, cc):
        return zz * 4 + yy * 2 + cc

    evo_copy = pltpu.make_async_copy(evo_hbm, gat.at[z, y, c], local_sem.at[0])
    prm_copy = pltpu.make_async_copy(prm_hbm, prm_ref, local_sem.at[1])
    scls_copy = pltpu.make_async_copy(scls_hbm, scls_in, local_sem.at[2])
    obs_copy = pltpu.make_async_copy(obs_hbm, obs, local_sem.at[3])
    sharp_copy = pltpu.make_async_copy(sharp_hbm, sharp_in, local_sem.at[4])
    ocls_copy = pltpu.make_async_copy(ocls_hbm, ocls_in, local_sem.at[5])
    pat_copy = pltpu.make_async_copy(pat_hbm, pat_ref, local_sem.at[6])

    has_up = z < depth - 1
    has_dn = z > 0
    barrier = pltpu.get_barrier_semaphore()

    def greet(dev):
        pl.semaphore_signal(barrier, inc=1, device_id={"blk": dev}, device_id_type=MESH)

    @pl.when(has_up)
    def _():
        greet(blk_of(z + 1, y, c))

    @pl.when(y == 0)
    def _():
        greet(blk_of(z, 1, c))

    @pl.when(c == 0)
    def _():
        greet(blk_of(z, y, 1))

    evo_copy.start()
    prm_copy.start()
    scls_copy.start()

    def is_end(o):
        return (o == 0) | (o == depth - 1)

    def remote(src, dst, dev, send, recv):
        return pltpu.make_async_remote_copy(
            src_ref=src,
            dst_ref=dst,
            send_sem=send,
            recv_sem=recv,
            device_id={"blk": dev},
            device_id_type=MESH,
        )

    def part(o, yy, cc, first, count, own):
        dst = gat.at[o, yy, cc, pl.ds(first, count)]
        return (evo_hbm.at[pl.ds(first, count)] if own else dst), dst

    def along_z(o, slot, own, zz, send):
        if slot == 4:
            src = dst = aux.at[o, y, c]
        elif slot > 4:
            src, dst = part(o, 1 - y, c, (2 * slot - 9) * quarter, quarter, False)
        else:
            src, dst = part(o, y, c, slot * quarter, quarter, own)
        k = o * 7 + slot
        return remote(src, dst, blk_of(zz, y, c), send.at[k], z_recv.at[k])

    def to_up(o, slot, own=False):
        return along_z(o, slot, own, z + 1, up_send)

    def to_dn(o, slot, own=False):
        return along_z(o, slot, own, z - 1, dn_send)

    def across_y(o, yy, slot, own):
        if slot == 4:
            src = dst = aux.at[o, yy, c]
        else:
            src, dst = part(o, yy, c, slot * quarter, quarter, own)
        k = o * 5 + slot
        return remote(src, dst, blk_of(z, 1 - y, c), y_send.at[k], y_recv.at[k])

    def to_y(o, slot, own=False):
        return across_y(o, y, slot, own)

    def from_y(o, slot):
        return across_y(o, 1 - y, slot, False)

    def core_hop(o, yy, cc, slot, own):
        if isinstance(slot, int) and slot == 2:
            src = dst = aux.at[o, yy, cc]
        else:
            src, dst = part(o, yy, cc, slot * half, half, own)
        k = (o * 2 + yy) * 3 + slot
        return remote(src, dst, blk_of(z, y, 1 - c), s_send.at[k], s_recv.at[k])

    def to_core(o, yy, slot, own=False):
        return core_hop(o, yy, c, slot, own)

    def from_core(o, yy, slot):
        return core_hop(o, yy, 1 - c, slot, False)

    def tell(k, dev):
        pl.semaphore_signal(ready.at[k], inc=1, device_id={"blk": dev}, device_id_type=MESH)

    def own_z(to, slots):
        for slot in slots:
            to(z, slot, True).start()

    def own_y(first, last):
        @pl.when(is_end(z))
        def _():
            for slot in (1, 0, 4, 3, 2)[first:last]:
                to_y(z, slot, True).start()

        @pl.when(jnp.logical_not(is_end(z)))
        def _():
            for slot in (0, 1, 4, 2, 3)[first:last]:
                to_y(z, slot, True).start()

    nearer = (z + depth - 1) // depth + y + c

    @pl.when(nearer > 0)
    def _():
        pl.semaphore_wait(barrier, nearer)

    @pl.when(has_dn)
    def _():
        own_z(to_dn, (0, 1))
        tell(0, blk_of(z - 1, y, c))

    @pl.when(y == 1)
    def _():
        own_y(0, 2)
        tell(1, blk_of(z, 0, c))

    @pl.when(c == 1)
    def _():
        tell(2, blk_of(z, y, 0))

    for copy in (obs_copy, sharp_copy, ocls_copy, pat_copy):
        copy.start()

    stage[...] = jnp.zeros_like(stage)
    prm_copy.wait()
    stage[0:nparam, :] = prm_ref[...].astype(jnp.float32)
    scls_copy.wait()
    stage[nparam : nparam + 1, :] = scls_in[...].reshape(1, sims).astype(jnp.float32)
    evo_copy.wait()
    block = gat[z, y, c].astype(jnp.float32)
    own_sq = 0.5 * jnp.sum(block * block, axis=1, keepdims=True)
    left = jnp.broadcast_to(own_sq, (LANES, LANES)).T[0:1, :]
    for k in range(3):
        piece = left.astype(jnp.bfloat16).astype(jnp.float32)
        stage[nparam + 1 + k : nparam + 2 + k, :] = piece
        left = left - piece
    aux[z, y, c] = stage[...].astype(jnp.bfloat16)

    @pl.when(has_dn)
    def _():
        own_z(to_dn, (4, 2, 3))

    @pl.when(y == 1)
    def _():
        own_y(2, 5)

    @pl.when(has_up)
    def _():
        pl.semaphore_wait(ready.at[0], 1)
        own_z(to_up, (0, 1, 4, 2, 3))

    @pl.when(y == 0)
    def _():
        pl.semaphore_wait(ready.at[1], 1)
        own_y(0, 5)

    @pl.when(c == 0)
    def _():
        pl.semaphore_wait(ready.at[2], 1)

    for slot in range(3):
        to_core(z, y, slot, True).start()

    sharp_copy.wait()
    ocls_copy.wait()
    pat_copy.wait()
    obs_copy.wait()
    for i in range(rows // LANES):
        lanes = slice(i * LANES, (i + 1) * LANES)
        sharp_ref[0:1, lanes] = (2.0 * LOG2_E) * sharp_in[lanes].reshape(1, LANES)
        ocls_ref[0:1, lanes] = ocls_in[lanes].reshape(1, LANES)
        turned = obs[lanes, :].T
        obs_t[:, lanes] = turned
        wide = turned.astype(jnp.float32)
        base_sc[0:1, lanes] = 1.0 * feat - 0.5 * jnp.sum(wide * wide, axis=0, keepdims=True)

    max_sc[...] = jnp.full_like(max_sc, NEG_START)
    tot_sc[...] = jnp.zeros_like(tot_sc)
    sum_sc[...] = jnp.zeros_like(sum_sc)

    first_half = lax.broadcasted_iota(jnp.int32, (AUX_ROWS, LANES), 1) < half

    def pair(*chunks):
        rows_in, packets, sources = [], [], []
        for place, (o, yy, cc, h) in enumerate(chunks):
            rows_in.append(gat[o, yy, cc, pl.ds(pl.multiple_of(h * half, half), half), :])
            packet = aux[o, yy, cc].astype(jnp.float32)
            packets.append(jnp.where(h == place, packet, pltpu.roll(packet, half, 1)))
            sources.append((blk_of(o, yy, cc), half))
        return rows_in, jnp.where(first_half, packets[0], packets[1]), sources

    def whole(o, yy, cc):
        return [gat[o, yy, cc]], aux[o, yy, cc].astype(jnp.float32), [(blk_of(o, yy, cc), sims)]

    def absorb(*parts):
        lhs, half_sq, classes, params = [], [], [], []
        for rows_in, packet, _ in parts:
            lhs.extend(rows_in)
            params.append(packet)
            column = packet[0:8, :].T
            classes.append(column[:, nparam : nparam + 1])
            half_sq.append(
                column[:, nparam + 1 : nparam + 2]
                + column[:, nparam + 2 : nparam + 3]
                + column[:, nparam + 3 : nparam + 4]
            )
        product = lax.dot_general(
            jnp.concatenate(lhs, axis=0),
            obs_t[...],
            (((1,), (0,)), ((), ())),
            preferred_element_type=jnp.float32,
        )
        sharp2 = sharp_ref[...]
        base = base_sc[...]
        masked = []
        for p, (_, _, sources) in enumerate(parts):
            row = 0
            for source, count in sources:
                wanted = jnp.concatenate(
                    [
                        jnp.where(
                            pat_ref[i, source] == 1,
                            ocls_ref[0:1, i * tile_rows : (i + 1) * tile_rows],
                            -1,
                        )
                        for i in range(tile_count)
                    ],
                    axis=1,
                ).astype(jnp.float32)
                mine = slice(row, row + count)
                span = slice(p * sims + row, p * sims + row + count)
                score = ((product[span] - half_sq[p][mine]) + base) * sharp2
                masked.append(jnp.where(classes[p][mine] == wanted, score, NEG_MASK))
                row += count
        top = functools.reduce(jnp.maximum, masked)
        old = max_sc[...]
        new = jnp.maximum(old, jnp.max(top, axis=0, keepdims=True))
        factor = jnp.exp2(old - new)
        weights = [jnp.exp2(m - new) for m in masked]
        max_sc[...] = new
        tot_sc[...] = tot_sc[...] * factor + jnp.sum(sum(weights), axis=0, keepdims=True)
        added = lax.dot_general(
            jnp.concatenate(params, axis=1).astype(jnp.bfloat16),
            jnp.concatenate(weights, axis=0).astype(jnp.bfloat16),
            (((1,), (0,)), ((), ())),
            preferred_element_type=jnp.float32,
        )
        sum_sc[...] = sum_sc[...] * factor + added

    def drain_z(o, slot):
        @pl.when(has_up & (o <= z))
        def _():
            to_up(o, slot).wait_send()

        @pl.when(has_dn & (o >= z))
        def _():
            to_dn(o, slot).wait_send()

    def drain(o):
        for slot in range(5):
            drain_z(o, slot)

        @pl.when(is_end(o))
        def _():
            drain_z(o, 5)
            drain_z(o, 6)

        @pl.when(jnp.logical_not(is_end(o)) | (o == z))
        def _():
            to_y(o, 1).wait_send()
            to_y(o, 3).wait_send()

        for slot in (0, 2, 4):
            to_y(o, slot).wait_send()
        for slot in range(3):
            to_core(o, y, slot).wait_send()
            to_core(o, 1 - y, slot).wait_send()

    def sides(dist):
        lo, hi = z - dist, z + dist
        return (
            (lo, (lo >= 0) & (dist >= 0), has_up, to_up),
            (hi, (hi < depth) & (dist > 0), has_dn, to_dn),
        )

    def pass_on(o, slot, further, to):
        to(o, slot).wait_recv()

        @pl.when(further)
        def _():
            to(o, slot).start()

    def same_row(s, q):
        for o, there, further, to in sides(s):

            @pl.when(there)
            def _():
                pass_on(o, q, further, to)
                if q % 2:

                    @pl.when(jnp.logical_not(is_end(o)))
                    def _():
                        to_y(o, q).start()

                    to_core(o, y, q // 2).start()
                else:
                    to_y(o, q).start()
                if q == 1:
                    pass_on(o, 4, further, to)
                    to_y(o, 4).start()
                    to_core(o, y, 2).start()

    def other_row(s, q):
        for o, there, _, to in sides(s - 1):

            @pl.when(there & is_end(o) & (o != z))
            def _():
                if q < 2:
                    from_y(o, 2 * q).wait_recv()
                    if q == 0:
                        from_y(o, 4).wait_recv()
                        to_core(o, 1 - y, 2).start()

                    @pl.when(is_end(z))
                    def _():
                        to(o, 5 + q).wait_recv()

                    to_core(o, 1 - y, q).start()

            @pl.when(there & jnp.logical_not(is_end(o)))
            def _():
                from_y(o, q).wait_recv()
                if q % 2:
                    to_core(o, 1 - y, q // 2).start()
                if q == 1:
                    from_y(o, 4).wait_recv()
                    to_core(o, 1 - y, 2).start()

            @pl.when(there & is_end(o) & (o == z))
            def _():
                from_y(o, (1, 0, 3, 2)[q]).wait_recv()
                if q % 2:
                    to_core(o, 1 - y, q // 2).start()
                else:

                    @pl.when(has_up)
                    def _():
                        to_up(o, 5 + q // 2).start()

                    @pl.when(has_dn)
                    def _():
                        to_dn(o, 5 + q // 2).start()

                if q == 1:
                    from_y(o, 4).wait_recv()
                    to_core(o, 1 - y, 2).start()

    def cross(s, q):
        for o, there, further, to in sides(s):

            @pl.when(there & is_end(o) & (o != z) & further)
            def _():
                to(o, 5 + q).wait_recv()
                to(o, 5 + q).start()

    def settle(dist):
        for o, there, _, _ in sides(dist):

            @pl.when(there)
            def _():
                drain(o)

    def fetch(o, yy, h):
        from_core(o, yy, h).wait_recv()

        @pl.when(h == 0)
        def _():
            from_core(o, yy, 2).wait_recv()

    far = depth - 1 - z
    before = z + (depth - 2) * (1 - 2 * (z // (depth - 1)))

    def turn(i, carry):
        s, q = 1 + i // 4, i % 4
        side, second = q % 2, q // 2
        inner = jnp.where(is_end(z), 0, 1)
        for k in range(4):

            @pl.when(q == k)
            def _():
                if k == 0:
                    settle(s - 3)
                same_row(s, k)
                if k < 2:
                    cross(s - 1, k)

        dist = jnp.where(inner == 1, s - 1, s - 1 + second)
        h = jnp.where(inner == 1, second, 1 - second)
        sign = 2 * side - 1
        row_o, other_o = z + sign * dist, z + sign * (dist - 1)
        row_ok = (row_o >= 0) & (row_o < depth) & ((dist > 0) | (q == 0))
        near = (dist > 1) | (side == (depth - 1 - z) // (depth - 1))
        other_ok = (other_o >= 0) & (other_o < depth) & (dist > 0) & near
        closing = (dist == depth) & is_end(z)
        ending = (s == depth) & is_end(z)
        last = ending & (q == 1)
        both = row_ok & other_ok & jnp.logical_not(ending)
        alone = (row_ok | other_ok) & jnp.logical_not(both | closing | ending)

        for k in range(2):

            @pl.when((q == 2 * k + 1) & (inner == 0) & (s < depth))
            def _():
                other_row(s, 2 * k)
                other_row(s, 2 * k + 1)

        @pl.when(last)
        def _():
            absorb(pair((far, y, c, 1), (before, 1 - y, c, 1)))
            other_row(s, 0)
            from_core(far, y, 1).wait_recv()
            from_core(before, 1 - y, 1).wait_recv()
            absorb(pair((far, y, 1 - c, 1), (before, 1 - y, 1 - c, 1)))
            other_row(s, 1)
            absorb(whole(far, 1 - y, c))

        one_at = jnp.where(row_ok, row_o, other_o)
        one_y = jnp.where(row_ok, y, 1 - y)
        two_at = jnp.where(both, other_o, one_at)
        two_y = jnp.where(both, 1 - y, one_y)
        two_h = jnp.where(both, h, 1 - h)
        usual = (both | (alone & ((h == 1) | (dist == 0)))) & jnp.logical_not(last)

        @pl.when(usual)
        def _():
            fetch(one_at, one_y, h)
            fetch(two_at, two_y, two_h)

        @pl.when(usual)
        def _():
            absorb(
                pair((one_at, one_y, 0, h), (one_at, one_y, 1, h)),
                pair((two_at, two_y, 0, two_h), (two_at, two_y, 1, two_h)),
            )

        @pl.when((q == 1) & (inner == 1))
        def _():
            other_row(s - 1, 2)
            other_row(s - 1, 3)

        @pl.when((q == 3) & (inner == 1))
        def _():
            other_row(s, 0)
            other_row(s, 1)

        return carry

    lax.fori_loop(0, 4 * depth, turn, 0)

    @pl.when(is_end(z))
    def _():
        settle(depth - 2)
        for slot in range(3):
            from_core(far, 1 - y, slot).wait_recv()
        absorb(whole(far, 1 - y, 1 - c))
        settle(depth - 1)

    @pl.when(jnp.logical_not(is_end(z)))
    def _():
        settle(depth - 2)

    out_ref[0:nparam, :] = sum_sc[0:nparam, :]
    out_ref[nparam : nparam + 1, :] = max_sc[...]
    out_ref[nparam + 1 : nparam + 2, :] = tot_sc[...]


def finish(state, mean_ref, lev_ref):
    nparam, rows = mean_ref.shape
    total = state[nparam + 1 : nparam + 2, :]
    mean_ref[...] = state[0:nparam, :] / total
    lev = state[nparam : nparam + 1, :] * LN_2 + jnp.log(total)
    for i in range(rows // LANES):
        lanes = slice(i * LANES, (i + 1) * LANES)
        lev_ref[lanes] = lev[0:1, lanes].reshape(LANES)


def solution(mesh):
    depth = mesh.shape["blk"] // 4

    def on_device(observed, sharpness, obs_class, pattern, evolved, sim_params, sim_class):
        rows, feat = observed.shape
        sims = evolved.shape[0]
        nparam = sim_params.shape[0]
        vmem = pl.BlockSpec(memory_space=pltpu.VMEM)
        hbm = pl.BlockSpec(memory_space=pltpu.HBM)
        dma = pltpu.SemaphoreType.DMA
        arguments = (observed, sharpness, obs_class, pattern, evolved, sim_params, sim_class)
        state = pl.pallas_call(
            functools.partial(gather_and_absorb, depth),
            out_shape=pltpu.VMEM((8, rows), jnp.float32),
            in_specs=[hbm] * 7,
            out_specs=vmem,
            scratch_shapes=[
                pltpu.VMEM((depth, 2, 2, sims, feat), jnp.bfloat16),
                pltpu.VMEM((depth, 2, 2, AUX_ROWS, LANES), jnp.bfloat16),
                pltpu.VMEM((rows, feat), jnp.bfloat16),
                pltpu.VMEM((feat, rows), jnp.bfloat16),
                pltpu.VMEM((rows,), jnp.float32),
                pltpu.VMEM((rows,), jnp.int32),
                pltpu.SMEM(pattern.shape, jnp.int32),
                pltpu.VMEM((nparam, sims), jnp.bfloat16),
                pltpu.VMEM((sims,), jnp.int32),
                pltpu.VMEM((AUX_ROWS, LANES), jnp.float32),
                pltpu.VMEM((1, rows), jnp.float32),
                pltpu.VMEM((1, rows), jnp.int32),
                pltpu.VMEM((1, rows), jnp.float32),
                pltpu.VMEM((1, rows), jnp.float32),
                pltpu.VMEM((1, rows), jnp.float32),
                pltpu.VMEM((AUX_ROWS, rows), jnp.float32),
                dma((7,)),
                dma((7 * depth,)),
                dma((7 * depth,)),
                dma((7 * depth,)),
                dma((5 * depth,)),
                dma((5 * depth,)),
                dma((6 * depth,)),
                dma((6 * depth,)),
                pltpu.SemaphoreType.REGULAR((3,)),
            ],
            compiler_params=pltpu.CompilerParams(
                collective_id=0, has_side_effects=True, vmem_limit_bytes=40 << 20
            ),
        )(*(pltpu.with_memory_space_constraint(a, pltpu.HBM) for a in arguments))
        return pl.pallas_call(
            finish,
            out_shape=(
                jax.ShapeDtypeStruct((nparam, rows), jnp.float32),
                jax.ShapeDtypeStruct((rows,), jnp.float32),
            ),
            in_specs=[vmem],
            out_specs=(vmem, vmem),
            compiler_params=pltpu.CompilerParams(vmem_limit_bytes=4 << 20),
        )(pltpu.with_memory_space_constraint(state, pltpu.VMEM))

    placed = (
        P(("parts", "blk"), None),
        P(("parts", "blk")),
        P(("parts", "blk")),
        P(("parts", "blk"), None),
        P(("parts", "blk"), None),
        P(None, ("parts", "blk")),
        P(("parts", "blk")),
    )
    return jax.shard_map(
        on_device,
        mesh=mesh,
        in_specs=placed,
        out_specs=(P(None, ("parts", "blk")), P(("parts", "blk"))),
        check_vma=False,
    )
```
